256 devices in a mesh: section: 4 (over z_hi), seq: 64 (over x, y, z_lo, core).
Axes of the slice: x: 4, y: 4, z: 8 (z_hi: 4, z_lo: 2; z = z_hi * 2 + z_lo), core: 2. Of those that a mesh axis runs over, the one named last changes fastest.
Arguments:
- memory: bfloat16 [8, 4096, 4096], P(None, 'seq', 'section'), may hold values from -6 to 6
- kv_weight: bfloat16 [4096, 4096], P('seq', 'section'), may hold values from -0.09375 to 0.09375
- mem_lengths: int32 [8], replicated, may hold values from 1024 to 4096, as said below
- queries: bfloat16 [16384, 2048], P('seq', 'section'), may hold values from -128 to 128
- out_weight: bfloat16 [2048, 4096], P('section'), may hold values from -0.125 to 0.125
- residual: bfloat16 [16384, 4096], P(('seq', 'section')), may hold values from -1.5 to 1.5
- norm_gain: float32 [4096], replicated, may hold values from 0.5 to 1.5
Outputs:
- hidden_out: bfloat16 [16384, 4096], P(('seq', 'section'))
- normed_out: bfloat16 [16384, 4096], P(('seq', 'section'))
The draws below stay inside these ranges and needn't reach their ends.
Inputs may be any that keep to these rules, and one draw needn't show every extreme that they name: `mem_lengths`: valid memory positions of each proof state; positions at or beyond it are padding; at least one proof state has none.
All inputs are finite; a program needn't handle non-finite values.
Results may differ from the reference program's by a relative error of at most 0.012.
Values may be sent and summed in bfloat16 or wider, within the bound.
No kernel may reach another device: no remote copies, remote signals or barrier semaphores. Data moves between devices by JAX's collectives and lax.ppermute only.
A program may use at most 128 MiB of HBM per device.

```python
import math
import jax
import jax.numpy as jnp
from jax import lax

D = 4096
DH = 256
HEADS = 8
STATES = 8
MEM = 4096
CT = 2048
HD = 2048


def draw_mem_lengths(key, part):
    len_key, pick_key = jax.random.split(key)
    lengths = jax.random.randint(len_key, (STATES,), MEM // 4, MEM + 1)
    full_state = jax.random.randint(pick_key, (), 0, STATES)
    return jnp.where(jnp.arange(STATES) == full_state, MEM, lengths).astype(jnp.int32)


def draw_queries(key, part):
    base_key = jax.random.fold_in(jax.random.fold_in(key, 7), 0)
    rows = STATES * CT
    values = jnp.clip(2.0 * jax.random.normal(base_key, (rows, HD), jnp.float32), -8.0, 8.0)
    return values.astype(jnp.bfloat16)


def level_of(rng, extent, cuts, smallest, high):
    gain, own = 1.0, jax.random.fold_in(rng, 6)
    for position, blocks in cuts:
        draws = jnp.exp(jax.random.uniform(jax.random.fold_in(own, position), (blocks,), jnp.float32, smallest / len(cuts), high / len(cuts)))
        gain = gain * jnp.repeat(draws, extent[position] // blocks).reshape([-1 if axis == position else 1 for axis in range(len(extent))])
    return gain


def normal_values(key, shape, scale, reach, cuts=(), kind=jnp.bfloat16):
    values = jax.random.normal(key, shape, jnp.float32) * scale
    if len(cuts) > 0:
        values = level_of(key, shape, cuts, -0.22, 0.18) * values
    return jnp.clip(values, min=-reach, max=reach).astype(kind)


def setup_inputs(seed: int = 0) -> dict:
    keys = jax.random.split(jax.random.key(seed), 8)
    return {
        "memory": normal_values(keys[0], (STATES, MEM, D), 1.0, 6.0, ((1, 64), (2, 4))),
        "kv_weight": normal_values(keys[1], (D, 2 * HD), D ** -0.5, 0.09375, ((0, 64), (1, 4))),
        "mem_lengths": draw_mem_lengths(jax.random.fold_in(keys[7], 71), 0),
        "queries": draw_queries(jax.random.fold_in(keys[7], 71), 0),
        "out_weight": normal_values(keys[4], (HD, D), HD ** -0.5, 0.125, ((0, 4),)),
        "residual": normal_values(keys[5], (STATES * CT, D), 0.25, 1.5, ((0, 256),)),
        "norm_gain": jnp.clip(1.0 + 0.1 * jax.random.normal(keys[6], (D,), jnp.float32), 0.5, 1.5),
    }


def reference(memory, kv_weight, mem_lengths, queries, out_weight, residual, norm_gain):
    score_scale = 1.0 / math.sqrt(DH)
    positions = jnp.arange(MEM, dtype=jnp.int32)
    query_states = queries.reshape(STATES, CT, HD)
    resid_states = residual.reshape(STATES, CT, D)

    def one_state(inputs):
        state_rows, length, query_rows, resid_rows = inputs
        key_value = jnp.dot(state_rows, kv_weight, preferred_element_type=jnp.float32).astype(jnp.bfloat16)
        split_heads = key_value.reshape(MEM, HEADS, 2, DH).astype(jnp.float32)
        query_per_head = query_rows.reshape(CT, HEADS, DH).astype(jnp.float32)
        logit_scores = jnp.einsum('wac,oac->awo', query_per_head, split_heads[:, :, 0, :]) * score_scale
        visible = positions < length.astype(jnp.int32)
        logit_scores = jnp.where(visible[None, None, :], logit_scores, -1e+30)
        highest = lax.optimization_barrier(jnp.max(logit_scores, axis=-1, keepdims=True))
        expo = jnp.exp(logit_scores - highest)
        softmax_weight = (expo / lax.optimization_barrier(jnp.sum(expo, axis=-1, keepdims=True))).astype(jnp.bfloat16)
        attended_context = jnp.einsum('fsw,wfy->sfy', softmax_weight.astype(jnp.float32), split_heads[:, :, 1, :])
        attended_context = attended_context.astype(jnp.bfloat16).reshape(CT, HD)
        attended = jnp.dot(attended_context, out_weight, preferred_element_type=jnp.float32)
        combined = resid_rows.astype(jnp.float32) + attended
        mean_square = lax.optimization_barrier(jnp.mean(combined * combined, axis=-1, keepdims=True))
        normed = combined * lax.rsqrt(mean_square + 1e-06) * norm_gain
        return (combined.astype(jnp.bfloat16), normed.astype(jnp.bfloat16))
    hidden_out, normed_out = lax.map(one_state, (memory, mem_lengths, query_states, resid_states))
    return (hidden_out.reshape(STATES * CT, D), normed_out.reshape(STATES * CT, D))
```

```python
import functools
import math

import jax
import jax.numpy as jnp
from jax import lax
from jax.experimental import pallas as pl
from jax.experimental.pallas import tpu as pltpu
from jax.sharding import Mesh, PartitionSpec as P


DH = 256
CHUNKS = 2
BF = jnp.bfloat16
F32 = jnp.float32
X = "x"
Y = ("yh", "yl")
Z = "zh"
EXP_SCALE = math.log2(math.e) / math.sqrt(DH)
FWD = [(i, (i + 1) % 4) for i in range(4)]
BWD = [(i, (i + 3) % 4) for i in range(4)]


def swap(a, axis):
    return lax.ppermute(a, axis, [(0, 1), (1, 0)])


def ring_pieces(a, axis):
    half = a.shape[0] // 2
    prev = lax.ppermute(a, axis, FWD)
    nxt = lax.ppermute(a, axis, BWD)
    opp_a = lax.ppermute(prev[:half], axis, FWD)
    opp_b = lax.ppermute(nxt[half:], axis, BWD)
    return nxt, opp_a, opp_b, prev


def ring(a, axis):
    nxt, opp_a, opp_b, prev = ring_pieces(a, axis)
    return jnp.concatenate([a, nxt, opp_a, opp_b, prev], 0).reshape((4,) + a.shape)


def pair(a, b, index):
    return jnp.where(index == 0, jnp.concatenate([a, b], 0), jnp.concatenate([b, a], 0))


def pick(a, b, index):
    return jnp.where(index == 0, a, b)


def project_kernel(where_ref, own, nxt, opp_a, opp_b, prev, wk, wv, wk_o, wv_o, out_own, out_oth, buf, sem):
    zh, x, y = where_ref[0], where_ref[1], where_ref[2]
    weights = (wk, wv, wk_o, wv_o)
    copies = [pltpu.make_async_copy(w, buf.at[i], sem.at[i]) for i, w in enumerate(weights)]
    for copy in copies:
        copy.start()
    half = own.shape[0] // 2
    for i in range(4):
        copies[i].wait()
        top = jnp.zeros((half, DH), F32)
        low = jnp.zeros((half, DH), F32)
        for dy in range(4):
            cols = pl.ds(pl.multiple_of(lax.rem(y + dy, 4) * DH, DH), DH)
            for dz in range(4):
                dx = lax.rem(zh + dz + 4 - x, 4)
                w = buf[i, dy, dx] if i % 2 == 0 else buf[i, dx, dy]
                if dz == 2:
                    a, b = opp_a[:, cols], opp_b[:, cols]
                else:
                    rows = (own, nxt, None, prev)[dz][:, cols]
                    a, b = rows[:half], rows[half:]
                top += jnp.dot(a, w, preferred_element_type=F32)
                low += jnp.dot(b, w, preferred_element_type=F32)
        out = out_own if i < 2 else out_oth
        at = (i % 2) * DH
        out[:half, at : at + DH] = top.astype(BF)
        out[half:, at : at + DH] = low.astype(BF)


def project(where, pieces, weights):
    rows = pieces[0].shape[0]
    vmem = pl.BlockSpec(memory_space=pltpu.VMEM)
    return pl.pallas_call(
        project_kernel,
        out_shape=[jax.ShapeDtypeStruct((rows, 2 * DH), BF)] * 2,
        in_specs=[pl.BlockSpec(memory_space=pltpu.SMEM)] + [vmem] * 5 + [pl.BlockSpec(memory_space=pl.ANY)] * 4,
        out_specs=[vmem] * 2,
        scratch_shapes=[pltpu.VMEM((4,) + weights[0].shape, BF), pltpu.SemaphoreType.DMA((4,))],
        name="project",
    )(where, *pieces, *weights)


def attend_kernel(chunk_rows, where_ref, q_ref, *refs):
    kv_refs, out_ref, bias_ref = refs[:-2], refs[-2], refs[-1]
    length, base, core = where_ref[0], where_ref[1], where_ref[2]
    per = chunk_rows // 16

    @pl.when(pl.program_id(0) == 0)
    def _():
        for j in range(len(kv_refs)):
            row = lax.broadcasted_iota(jnp.int32, (chunk_rows, 128), 0)
            source = row // (2 * per)
            side = (row // per) % 2
            position = source * 512 + base + (side ^ core) * 64 + j * per + row % per
            bias_ref[pl.ds(j * chunk_rows, chunk_rows), :] = jnp.where(position < length, 0.0, -1e30)

    q = q_ref[...]
    scores = []
    for j, kv in enumerate(kv_refs):
        s = lax.dot_general(kv[:, :DH], q, (((1,), (1,)), ((), ())), preferred_element_type=F32)
        bias = bias_ref[pl.ds(j * chunk_rows, chunk_rows), :]
        scores.append(s + jnp.concatenate([bias] * (q.shape[0] // 128), axis=1))
    high = functools.reduce(jnp.maximum, [jnp.max(s, axis=0, keepdims=True) for s in scores])
    total = jnp.zeros_like(high)
    acc = jnp.zeros((DH, q.shape[0]), F32)
    for s, kv in zip(scores, kv_refs):
        p = jnp.exp2((s - high) * EXP_SCALE)
        total += jnp.sum(p, axis=0, keepdims=True)
        acc += lax.dot_general(kv[:, DH:], p.astype(BF), (((0,), (0,)), ((), ())), preferred_element_type=F32)
    out_ref[0, :DH] = (acc / total).astype(BF)
    lse = high * EXP_SCALE + jnp.log2(total)
    first = lse.astype(BF)
    rest = lse - first.astype(F32)
    second = rest.astype(BF)
    third = (rest - second.astype(F32)).astype(BF)
    zero = jnp.zeros((13, q.shape[0]), F32)
    stats = jnp.concatenate([first.astype(F32), second.astype(F32), third.astype(F32), zero], 0)
    out_ref[0, DH:] = stats.astype(BF)


def attend(where, q, kvs):
    rows = kvs[0].shape[0]
    tokens = q.shape[0]
    whole = pl.BlockSpec((rows, 2 * DH), lambda i: (0, 0))
    return pl.pallas_call(
        functools.partial(attend_kernel, rows),
        grid=(tokens // 256,),
        out_shape=jax.ShapeDtypeStruct((tokens // 256, DH + 16, 256), BF),
        in_specs=[pl.BlockSpec(memory_space=pltpu.SMEM), pl.BlockSpec((256, DH), lambda i: (i, 0))] + [whole] * len(kvs),
        out_specs=pl.BlockSpec((1, DH + 16, 256), lambda i: (i, 0, 0)),
        scratch_shapes=[pltpu.VMEM((rows * len(kvs), 128), F32)],
        name="attend",
    )(where, q, *kvs)


def merge_kernel(part_ref, out_ref):
    for head in range(2):
        stats = [part_ref[2 * j + head, DH:].astype(F32) for j in range(4)]
        lse = [s[0:1] + s[1:2] + s[2:3] for s in stats]
        high = functools.reduce(jnp.maximum, lse)
        weight = [jnp.exp2(v - high) for v in lse]
        inverse = 1.0 / sum(weight)
        context = sum(part_ref[2 * j + head, :DH].astype(F32) * (weight[j] * inverse) for j in range(4))
        context = context.T.astype(BF)
        for m in range(4):
            out_ref[m, :, head * DH : (head + 1) * DH] = context[m * 64 : (m + 1) * 64]


def merge(parts):
    vmem = pl.BlockSpec(memory_space=pltpu.VMEM)
    return pl.pallas_call(
        merge_kernel,
        out_shape=jax.ShapeDtypeStruct((4, 64, 2 * DH), BF),
        in_specs=[vmem],
        out_specs=vmem,
        name="merge",
    )(parts)


def output_kernel(where_ref, own, oth, wa_ref, wb_ref, out_own, out_oth):
    zh, x, y = where_ref[0], where_ref[1], where_ref[2]
    step = pl.program_id(0)
    dx, dy = step // 2, (step % 2) * 2
    acc = jnp.zeros((128, 256), F32)
    for k in range(4):
        section = lax.rem(zh + k, 4)
        rows = jnp.concatenate([own[section], oth[section]], 0)
        if k < 2:
            w = jnp.concatenate([wa_ref[0, 0, k], wa_ref[1, 0, k]], 1)
        else:
            w = jnp.concatenate([wb_ref[0, 0, k - 2], wb_ref[0, 1, k - 2]], 1)
        acc += jnp.dot(rows, w, preferred_element_type=F32)
    for i in range(2):
        block = lax.rem(x + dx, 4) * 4 + lax.rem(y + dy + i, 4)
        cols = pl.ds(pl.multiple_of(block * 128, 128), 128)
        out_own[:, cols] = acc[:64, i * 128 : (i + 1) * 128]
        out_oth[:, cols] = acc[64:, i * 128 : (i + 1) * 128]


def output(where, own, oth, wa, wb):
    whole = pl.BlockSpec((4, 64, 2 * DH), lambda i: (0, 0, 0))
    out = pl.BlockSpec((64, 2048), lambda i: (0, 0))
    return pl.pallas_call(
        output_kernel,
        grid=(8,),
        out_shape=[jax.ShapeDtypeStruct((64, 2048), F32)] * 2,
        in_specs=[
            pl.BlockSpec(memory_space=pltpu.SMEM),
            whole,
            whole,
            pl.BlockSpec((2, 1, 2, 512, 128), lambda i: (i % 2, i // 2, 0, 0, 0)),
            pl.BlockSpec((1, 2, 2, 512, 128), lambda i: (i // 2, i % 2, 0, 0, 0)),
        ],
        out_specs=[out] * 2,
        name="output",
    )(where, own, oth, wa, wb)


def finish_kernel(c_ref, mine, other, residual, gain, hidden, normed):
    swapped = c_ref[0] == 1
    a, b = mine[...], other[...]
    low = residual[:, :2048].astype(F32) + jnp.where(swapped, b, a)
    high = residual[:, 2048:].astype(F32) + jnp.where(swapped, a, b)
    squares = jnp.sum(low * low, -1, keepdims=True) + jnp.sum(high * high, -1, keepdims=True)
    scale = lax.rsqrt(squares * (1.0 / 4096) + 1e-06)
    hidden[:, :2048] = low.astype(BF)
    hidden[:, 2048:] = high.astype(BF)
    normed[:, :2048] = (low * scale * gain[:, :2048]).astype(BF)
    normed[:, 2048:] = (high * scale * gain[:, 2048:]).astype(BF)


def finish(core, mine, other, residual, gain):
    vmem = pl.BlockSpec(memory_space=pltpu.VMEM)
    return pl.pallas_call(
        finish_kernel,
        out_shape=[jax.ShapeDtypeStruct(residual.shape, BF)] * 2,
        in_specs=[pl.BlockSpec(memory_space=pltpu.SMEM)] + [vmem] * 4,
        out_specs=[vmem] * 2,
        name="finish",
    )(core, mine, other, residual, gain)


def shards(memory, kv_weight, mem_lengths, queries, out_weight, residual, norm_gain):
    zh, x, yh, yl, zl, c = (lax.axis_index(a) for a in (Z, X, "yh", "yl", "zl", "c"))
    y = yh * 2 + yl
    where = jnp.stack([zh, x, y]).astype(jnp.int32)

    step = memory.shape[1] // CHUNKS
    chunks = []
    for j in range(CHUNKS):
        own = memory[:, j * step : (j + 1) * step].reshape(8 * step, 1024)
        chunks.append((own,) + ring_pieces(own, Z))

    mine = pick(kv_weight[:, :512], kv_weight[:, 512:], c)
    theirs = pick(kv_weight[:, 512:], kv_weight[:, :512], c)
    rows = pair(mine, swap(theirs, "c"), c)
    rows = pair(rows, swap(rows, "zl"), zl)
    wk = ring(ring(rows[:, :DH], X), Y)
    wv = ring(ring(rows[:, DH:], Y), X)
    weights = (wk, wv, swap(wk, "c"), swap(wv, "c"))

    q = pair(
        pick(queries[:, :DH], queries[:, DH:], c),
        swap(pick(queries[:, DH:], queries[:, :DH], c), "c"),
        c,
    )
    q = pair(q, swap(q, "zl"), zl)
    q = pair(q, swap(q, "yl"), yl)

    start = c * 2048 + (x * 4 + y) * 128
    ow = lax.dynamic_slice(out_weight, (zl * 256, start), (256, 128))
    ow = ring(ow, Z)
    other = swap(ow, "zl")
    ow = jnp.where(zl == 0, jnp.concatenate([ow, other], 1), jnp.concatenate([other, ow], 1))
    wa = ring(ring(ow[:2], X), Y)
    wb = ring(ring(ow[2:], Y), X)

    kvs = []
    for pieces in chunks:
        own, oth = project(where, pieces, weights)
        both = jnp.stack([own.reshape(8, step, 512), swap(oth, "c").reshape(8, step, 512)], 1)
        both = lax.all_to_all(both, (X, "yh"), 0, 0, tiled=True)
        kvs.append(both.reshape(16 * step, 512))

    length = lax.dynamic_index_in_dim(mem_lengths, x * 2 + yh, 0, keepdims=False)
    here = jnp.stack([length, yl * 256 + zl * 128, c]).astype(jnp.int32)
    part = attend(here, q, kvs)
    part = lax.all_to_all(part, ("yl", "zl", "c"), 0, 0, tiled=True)
    context = merge(part)
    context = lax.all_to_all(context, Z, 0, 0, tiled=True)
    mine, theirs = output(where, context, swap(context, "c"), wa, wb)
    other = swap(theirs, "c")
    return tuple(finish(c.reshape(1).astype(jnp.int32), mine, other, residual, norm_gain.reshape(1, -1)))


def solution(mesh):
    fine = Mesh(mesh.devices.reshape(4, 4, 2, 2, 2, 2), (Z, X, "yh", "yl", "zl", "c"))
    seq = (X, "yh", "yl", "zl", "c")
    in_specs = (
        P(None, seq, Z),
        P(seq, Z),
        P(),
        P(seq, Z),
        P(Z, None),
        P(seq + (Z,), None),
        P(),
    )
    out_specs = (P(seq + (Z,), None), P(seq + (Z,), None))
    return jax.shard_map(shards, mesh=fine, in_specs=in_specs, out_specs=out_specs, check_vma=False)
```

```python
import functools
import math

import jax
import jax.numpy as jnp
from jax import lax
from jax.experimental import pallas as pl
from jax.experimental.pallas import tpu as pltpu
from jax.sharding import Mesh, PartitionSpec as P


DH = 256
CHUNKS = 2
BF = jnp.bfloat16
F32 = jnp.float32
X = "x"
XY = ("x", "yh", "yl")
Z = "zh"
EXP_SCALE = math.log2(math.e) / math.sqrt(DH)
FWD = [(i, (i + 1) % 4) for i in range(4)]
BWD = [(i, (i + 3) % 4) for i in range(4)]


def swap(a, axis):
    return lax.ppermute(a, axis, [(0, 1), (1, 0)])


def ring_pieces(a, axis):
    half = a.shape[0] // 2
    prev = lax.ppermute(a, axis, FWD)
    nxt = lax.ppermute(a, axis, BWD)
    opp_a = lax.ppermute(prev[:half], axis, FWD)
    opp_b = lax.ppermute(nxt[half:], axis, BWD)
    return nxt, opp_a, opp_b, prev


def pair(a, b, index, axis=0):
    return jnp.where(index == 0, jnp.concatenate([a, b], axis), jnp.concatenate([b, a], axis))


def pick(a, b, index):
    return jnp.where(index == 0, a, b)


def project_kernel(where_ref, own, nxt, opp_a, opp_b, prev, w_mine, w_theirs, out_mine, out_theirs, buf, sem):
    zh = where_ref[0]
    copies = [
        pltpu.make_async_copy(w.at[:, pl.ds(i * DH, DH)], buf.at[2 * j + i], sem.at[2 * j + i])
        for j, w in enumerate((w_mine, w_theirs))
        for i in range(2)
    ]
    for copy in copies:
        copy.start()
    for i in range(4):
        copies[i].wait()
        acc = jnp.zeros((own.shape[0], DH), F32)
        for dz in range(4):
            if dz == 2:
                rows = jnp.concatenate([opp_a[...], opp_b[...]], 0)
            else:
                rows = (own, nxt, None, prev)[dz][...]
            block = pl.ds(pl.multiple_of(lax.rem(zh + dz, 4) * 1024, 1024), 1024)
            acc += jnp.dot(rows, buf[i, block], preferred_element_type=F32)
        out = out_mine if i < 2 else out_theirs
        out[:, (i % 2) * DH : (i % 2 + 1) * DH] = acc.astype(BF)


def project(where, pieces, weights):
    rows = pieces[0].shape[0]
    vmem = pl.BlockSpec(memory_space=pltpu.VMEM)
    return pl.pallas_call(
        project_kernel,
        out_shape=[jax.ShapeDtypeStruct((rows, 2 * DH), BF)] * 2,
        in_specs=[pl.BlockSpec(memory_space=pltpu.SMEM)] + [vmem] * 5 + [pl.BlockSpec(memory_space=pl.ANY)] * 2,
        out_specs=[vmem] * 2,
        scratch_shapes=[pltpu.VMEM((4, 4096, DH), BF), pltpu.SemaphoreType.DMA((4,))],
        name="project",
    )(where, *pieces, *weights)


def attend_kernel(chunk_rows, where_ref, q_ref, *refs):
    kv_refs, out_ref, bias_ref = refs[:-2], refs[-2], refs[-1]
    length, base = where_ref[0], where_ref[1]
    per = chunk_rows // 16

    @pl.when(pl.program_id(0) == 0)
    def _():
        for j in range(len(kv_refs)):
            row = lax.broadcasted_iota(jnp.int32, (chunk_rows, 128), 0)
            source = row // (2 * per)
            side = (row // per) % 2
            position = source * 512 + base + side * 64 + j * per + row % per
            bias_ref[pl.ds(j * chunk_rows, chunk_rows), :] = jnp.where(position < length, 0.0, -1e30)

    q = q_ref[...]
    scores = []
    for j, kv in enumerate(kv_refs):
        s = lax.dot_general(kv[:, :DH], q, (((1,), (1,)), ((), ())), preferred_element_type=F32)
        bias = bias_ref[pl.ds(j * chunk_rows, chunk_rows), :]
        scores.append(s + jnp.concatenate([bias] * (q.shape[0] // 128), axis=1))
    high = functools.reduce(jnp.maximum, [jnp.max(s, axis=0, keepdims=True) for s in scores])
    total = jnp.zeros_like(high)
    acc = jnp.zeros((DH, q.shape[0]), F32)
    for s, kv in zip(scores, kv_refs):
        p = jnp.exp2((s - high) * EXP_SCALE)
        total += jnp.sum(p, axis=0, keepdims=True)
        acc += lax.dot_general(kv[:, DH:], p.astype(BF), (((0,), (0,)), ((), ())), preferred_element_type=F32)
    out_ref[0, :DH] = (acc / total).astype(BF)
    lse = high * EXP_SCALE + jnp.log2(total)
    first = lse.astype(BF)
    rest = lse - first.astype(F32)
    second = rest.astype(BF)
    third = (rest - second.astype(F32)).astype(BF)
    zero = jnp.zeros((13, q.shape[0]), F32)
    stats = jnp.concatenate([first.astype(F32), second.astype(F32), third.astype(F32), zero], 0)
    out_ref[0, DH:] = stats.astype(BF)


def attend(where, q, kvs):
    rows = kvs[0].shape[0]
    tokens = q.shape[0]
    whole = pl.BlockSpec((rows, 2 * DH), lambda i: (0, 0))
    return pl.pallas_call(
        functools.partial(attend_kernel, rows),
        grid=(tokens // 256,),
        out_shape=jax.ShapeDtypeStruct((tokens // 256, DH + 16, 256), BF),
        in_specs=[pl.BlockSpec(memory_space=pltpu.SMEM), pl.BlockSpec((256, DH), lambda i: (i, 0))] + [whole] * len(kvs),
        out_specs=pl.BlockSpec((1, DH + 16, 256), lambda i: (i, 0, 0)),
        scratch_shapes=[pltpu.VMEM((rows * len(kvs), 128), F32)],
        name="attend",
    )(where, q, *kvs)


def merge_kernel(part_ref, out_ref):
    for head in range(2):
        stats = [part_ref[2 * j + head, DH:].astype(F32) for j in range(4)]
        lse = [s[0:1] + s[1:2] + s[2:3] for s in stats]
        high = functools.reduce(jnp.maximum, lse)
        weight = [jnp.exp2(v - high) for v in lse]
        inverse = 1.0 / sum(weight)
        context = sum(part_ref[2 * j + head, :DH].astype(F32) * (weight[j] * inverse) for j in range(4))
        context = context.T.astype(BF)
        for m in range(4):
            out_ref[m, :, head * DH : (head + 1) * DH] = context[m * 64 : (m + 1) * 64]


def merge(parts):
    vmem = pl.BlockSpec(memory_space=pltpu.VMEM)
    return pl.pallas_call(
        merge_kernel,
        out_shape=jax.ShapeDtypeStruct((4, 64, 2 * DH), BF),
        in_specs=[vmem],
        out_specs=vmem,
        name="merge",
    )(parts)


def output_kernel(own, oth, w_ref, out_own, out_oth):
    acc = jnp.zeros((128, w_ref.shape[1]), F32)
    for k in range(4):
        rows = jnp.concatenate([own[k], oth[k]], 0)
        acc += jnp.dot(rows, w_ref[k * 512 : (k + 1) * 512], preferred_element_type=F32)
    out_own[...] = acc[:64]
    out_oth[...] = acc[64:]


def output(own, oth, w):
    whole = pl.BlockSpec((4, 64, 2 * DH), lambda i: (0, 0, 0))
    out = pl.BlockSpec((64, 256), lambda i: (0, i))
    return pl.pallas_call(
        output_kernel,
        grid=(8,),
        out_shape=[jax.ShapeDtypeStruct((64, 2048), F32)] * 2,
        in_specs=[whole, whole, pl.BlockSpec((2048, 256), lambda i: (0, i))],
        out_specs=[out] * 2,
        name="output",
    )(own, oth, w)


def finish_kernel(c_ref, mine, other, residual, gain, hidden, normed):
    swapped = c_ref[0] == 1
    a, b = mine[...], other[...]
    low = residual[:, :2048].astype(F32) + jnp.where(swapped, b, a)
    high = residual[:, 2048:].astype(F32) + jnp.where(swapped, a, b)
    squares = jnp.sum(low * low, -1, keepdims=True) + jnp.sum(high * high, -1, keepdims=True)
    scale = lax.rsqrt(squares * (1.0 / 4096) + 1e-06)
    hidden[:, :2048] = low.astype(BF)
    hidden[:, 2048:] = high.astype(BF)
    normed[:, :2048] = (low * scale * gain[:, :2048]).astype(BF)
    normed[:, 2048:] = (high * scale * gain[:, 2048:]).astype(BF)


def finish(core, mine, other, residual, gain):
    vmem = pl.BlockSpec(memory_space=pltpu.VMEM)
    return pl.pallas_call(
        finish_kernel,
        out_shape=[jax.ShapeDtypeStruct(residual.shape, BF)] * 2,
        in_specs=[pl.BlockSpec(memory_space=pltpu.SMEM)] + [vmem] * 4,
        out_specs=[vmem] * 2,
        name="finish",
    )(core, mine, other, residual, gain)


def shards(memory, kv_weight, mem_lengths, queries, out_weight, residual, norm_gain):
    zh, x, yh, yl, zl, c = (lax.axis_index(a) for a in (Z, X, "yh", "yl", "zl", "c"))
    y = yh * 2 + yl
    where = jnp.stack([zh, x, y]).astype(jnp.int32)

    mine = pick(kv_weight[:, :512], kv_weight[:, 512:], c)
    theirs = pick(kv_weight[:, 512:], kv_weight[:, :512], c)
    rows = pair(mine, swap(theirs, "c"), c)
    rows = pair(rows, swap(rows, "zl"), zl)
    w_mine = lax.all_gather(rows, XY, axis=0, tiled=True)
    w_theirs = swap(w_mine, "c")

    step = memory.shape[1] // CHUNKS
    chunks = []
    for j in range(CHUNKS):
        own = memory[:, j * step : (j + 1) * step].reshape(8 * step, 1024)
        chunks.append((own,) + ring_pieces(own, Z))

    q = pair(
        pick(queries[:, :DH], queries[:, DH:], c),
        swap(pick(queries[:, DH:], queries[:, :DH], c), "c"),
        c,
    )
    q = pair(q, swap(q, "zl"), zl)
    q = pair(q, swap(q, "yl"), yl)

    start = c * 2048 + (x * 4 + y) * 128
    ow = lax.dynamic_slice(out_weight, (zl * 256, start), (256, 128))
    ow = lax.all_gather(ow, (Z, "zl"), axis=0, tiled=True)
    ow = lax.all_gather(ow, XY, axis=1, tiled=True)

    kvs = []
    for pieces in chunks:
        own, oth = project(where, pieces, (w_mine, w_theirs))
        both = pair(own.reshape(8, 1, step, 512), oth.reshape(8, 1, step, 512), c, 1)
        both = lax.all_to_all(both.reshape(16, step, 512), (X, "yh", "c"), 0, 0, tiled=True)
        kvs.append(both.reshape(16 * step, 512))

    length = lax.dynamic_index_in_dim(mem_lengths, x * 2 + yh, 0, keepdims=False)
    here = jnp.stack([length, yl * 256 + zl * 128]).astype(jnp.int32)
    part = attend(here, q, kvs)
    part = lax.all_to_all(part, ("yl", "zl", "c"), 0, 0, tiled=True)
    context = merge(part)
    context = lax.all_to_all(context, Z, 0, 0, tiled=True)
    mine, theirs = output(context, swap(context, "c"), ow)
    other = swap(theirs, "c")
    return tuple(finish(c.reshape(1).astype(jnp.int32), mine, other, residual, norm_gain.reshape(1, -1)))


def solution(mesh):
    fine = Mesh(mesh.devices.reshape(4, 4, 2, 2, 2, 2), (Z, X, "yh", "yl", "zl", "c"))
    seq = (X, "yh", "yl", "zl", "c")
    in_specs = (
        P(None, seq, Z),
        P(seq, Z),
        P(),
        P(seq, Z),
        P(Z, None),
        P(seq + (Z,), None),
        P(),
    )
    out_specs = (P(seq + (Z,), None), P(seq + (Z,), None))
    return jax.shard_map(shards, mesh=fine, in_specs=in_specs, out_specs=out_specs, check_vma=False)
```

```python
import functools
import math

import jax
import jax.numpy as jnp
from jax import lax
from jax.experimental import pallas as pl
from jax.experimental.pallas import tpu as pltpu
from jax.sharding import Mesh, PartitionSpec as P


DH = 256
CHUNKS = 2
BF = jnp.bfloat16
F32 = jnp.float32
X = "x"
XY = ("x", "yh", "yl")
Z = "zh"
EXP_SCALE = math.log2(math.e) / math.sqrt(DH)
FWD = [(i, (i + 1) % 4) for i in range(4)]
BWD = [(i, (i + 3) % 4) for i in range(4)]


def swap(a, axis):
    return lax.ppermute(a, axis, [(0, 1), (1, 0)])


def ring(a, axis):
    half = a.shape[0] // 2
    prev = lax.ppermute(a, axis, FWD)
    nxt = lax.ppermute(a, axis, BWD)
    opp_a = lax.ppermute(prev[:half], axis, FWD)
    opp_b = lax.ppermute(nxt[half:], axis, BWD)
    return nxt, jnp.concatenate([opp_a, opp_b], 0), prev


def pair(a, b, index, axis=0):
    return jnp.where(index == 0, jnp.concatenate([a, b], axis), jnp.concatenate([b, a], axis))


def pick(a, b, index):
    return jnp.where(index == 0, a, b)


def project_kernel(where_ref, own, nxt, opp_a, opp_b, prev, w_mine, w_theirs, out_mine, out_theirs, buf, sem):
    zh = where_ref[0]
    copies = []
    for dz in range(4):
        block = pl.ds(pl.multiple_of(lax.rem(zh + dz, 4) * 1024, 1024), 1024)
        for j, w in enumerate((w_mine, w_theirs)):
            copies.append(pltpu.make_async_copy(w.at[block], buf.at[2 * dz + j], sem.at[2 * dz + j]))
            copies[-1].start()
    acc = [jnp.zeros((own.shape[0], 2 * DH), F32)] * 2
    for dz in range(4):
        if dz == 2:
            rows = jnp.concatenate([opp_a[...], opp_b[...]], 0)
        else:
            rows = (own, nxt, None, prev)[dz][...]
        for j in range(2):
            copies[2 * dz + j].wait()
            acc[j] = acc[j] + jnp.dot(rows, buf[2 * dz + j], preferred_element_type=F32)
    out_mine[...] = acc[0].astype(BF)
    out_theirs[...] = acc[1].astype(BF)


def project(where, pieces, weights):
    rows = pieces[0].shape[0]
    vmem = pl.BlockSpec(memory_space=pltpu.VMEM)
    return pl.pallas_call(
        project_kernel,
        out_shape=[jax.ShapeDtypeStruct((rows, 2 * DH), BF)] * 2,
        in_specs=[pl.BlockSpec(memory_space=pltpu.SMEM)] + [vmem] * 5 + [pl.BlockSpec(memory_space=pl.ANY)] * 2,
        out_specs=[vmem] * 2,
        scratch_shapes=[pltpu.VMEM((8, 1024, 2 * DH), BF), pltpu.SemaphoreType.DMA((8,))],
        name="project",
    )(where, *pieces, *weights)


def attend_kernel(chunk_rows, where_ref, q_ref, *refs):
    kv_refs, out_ref, bias_ref = refs[:-2], refs[-2], refs[-1]
    length, base = where_ref[0], where_ref[1]
    per = chunk_rows // 16

    @pl.when(pl.program_id(0) == 0)
    def _():
        for j in range(len(kv_refs)):
            row = lax.broadcasted_iota(jnp.int32, (chunk_rows, 128), 0)
            source = row // (2 * per)
            side = (row // per) % 2
            position = source * 512 + base + side * 64 + j * per + row % per
            bias_ref[pl.ds(j * chunk_rows, chunk_rows), :] = jnp.where(position < length, 0.0, -1e30)

    q = q_ref[...]
    scores = []
    for j, kv in enumerate(kv_refs):
        s = lax.dot_general(kv[:, :DH], q, (((1,), (1,)), ((), ())), preferred_element_type=F32)
        bias = bias_ref[pl.ds(j * chunk_rows, chunk_rows), :]
        scores.append(s + jnp.concatenate([bias] * (q.shape[0] // 128), axis=1))
    high = functools.reduce(jnp.maximum, [jnp.max(s, axis=0, keepdims=True) for s in scores])
    total = jnp.zeros_like(high)
    acc = jnp.zeros((DH, q.shape[0]), F32)
    for s, kv in zip(scores, kv_refs):
        p = jnp.exp2((s - high) * EXP_SCALE)
        total += jnp.sum(p, axis=0, keepdims=True)
        acc += lax.dot_general(kv[:, DH:], p.astype(BF), (((0,), (0,)), ((), ())), preferred_element_type=F32)
    out_ref[0, :DH] = (acc / total).astype(BF)
    lse = high * EXP_SCALE + jnp.log2(total)
    first = lse.astype(BF)
    rest = lse - first.astype(F32)
    second = rest.astype(BF)
    third = (rest - second.astype(F32)).astype(BF)
    zero = jnp.zeros((13, q.shape[0]), F32)
    stats = jnp.concatenate([first.astype(F32), second.astype(F32), third.astype(F32), zero], 0)
    out_ref[0, DH:] = stats.astype(BF)


def attend(where, q, kvs):
    rows = kvs[0].shape[0]
    tokens = q.shape[0]
    whole = pl.BlockSpec((rows, 2 * DH), lambda i: (0, 0))
    return pl.pallas_call(
        functools.partial(attend_kernel, rows),
        grid=(tokens // 256,),
        out_shape=jax.ShapeDtypeStruct((tokens // 256, DH + 16, 256), BF),
        in_specs=[pl.BlockSpec(memory_space=pltpu.SMEM), pl.BlockSpec((256, DH), lambda i: (i, 0))] + [whole] * len(kvs),
        out_specs=pl.BlockSpec((1, DH + 16, 256), lambda i: (i, 0, 0)),
        scratch_shapes=[pltpu.VMEM((rows * len(kvs), 128), F32)],
        name="attend",
    )(where, q, *kvs)


def merge_kernel(a_ref, b_ref, c_ref, d_ref, out_ref):
    refs = (a_ref, b_ref, c_ref, d_ref)
    for side in range(2):
        stats = [ref[side, DH:].astype(F32) for ref in refs]
        lse = [s[0:1] + s[1:2] + s[2:3] for s in stats]
        high = functools.reduce(jnp.maximum, lse)
        weight = [jnp.exp2(v - high) for v in lse]
        inverse = 1.0 / sum(weight)
        context = sum(ref[side, :DH].astype(F32) * (w * inverse) for ref, w in zip(refs, weight))
        out_ref[side] = context.T.astype(BF)


def merge(parts):
    vmem = pl.BlockSpec(memory_space=pltpu.VMEM)
    return pl.pallas_call(
        merge_kernel,
        out_shape=jax.ShapeDtypeStruct((2, 256, DH), BF),
        in_specs=[vmem] * 4,
        out_specs=vmem,
        name="merge",
    )(*parts)


def output_kernel(where_ref, *refs):
    ctx, w_ref, out_own, out_oth, acc = refs[:8], refs[8], refs[9], refs[10], refs[11]
    k = pl.program_id(0)

    @pl.when(k == 0)
    def _():
        acc[...] = jnp.zeros_like(acc)

    rows = jnp.concatenate([ctx[0][...], ctx[1][...]], 0)
    for dz in range(1, 4):
        rows = jnp.where(k == dz, jnp.concatenate([ctx[2 * dz][...], ctx[2 * dz + 1][...]], 0), rows)
    acc[...] += jnp.dot(rows, w_ref[...], preferred_element_type=F32)

    @pl.when(k == 3)
    def _():
        out_own[...] = acc[:64]
        out_oth[...] = acc[64:]


def output(where, ctx, w):
    whole = pl.BlockSpec((64, 2 * DH), lambda i: (0, 0))
    out = pl.BlockSpec((64, 2048), lambda i: (0, 0))
    return pl.pallas_call(
        output_kernel,
        grid=(4,),
        out_shape=[jax.ShapeDtypeStruct((64, 2048), F32)] * 2,
        in_specs=[pl.BlockSpec(memory_space=pltpu.SMEM)] + [whole] * 8 + [pl.BlockSpec((512, 2048), lambda i: (i, 0))],
        out_specs=[out] * 2,
        scratch_shapes=[pltpu.VMEM((128, 2048), F32)],
        name="output",
    )(where, *ctx, w)


def finish_kernel(c_ref, mine, other, residual, gain, hidden, normed):
    swapped = c_ref[0] == 1
    a, b = mine[...], other[...]
    low = residual[:, :2048].astype(F32) + jnp.where(swapped, b, a)
    high = residual[:, 2048:].astype(F32) + jnp.where(swapped, a, b)
    squares = jnp.sum(low * low, -1, keepdims=True) + jnp.sum(high * high, -1, keepdims=True)
    scale = lax.rsqrt(squares * (1.0 / 4096) + 1e-06)
    hidden[:, :2048] = low.astype(BF)
    hidden[:, 2048:] = high.astype(BF)
    normed[:, :2048] = (low * scale * gain[:, :2048]).astype(BF)
    normed[:, 2048:] = (high * scale * gain[:, 2048:]).astype(BF)


def finish(core, mine, other, residual, gain):
    vmem = pl.BlockSpec(memory_space=pltpu.VMEM)
    return pl.pallas_call(
        finish_kernel,
        out_shape=[jax.ShapeDtypeStruct(residual.shape, BF)] * 2,
        in_specs=[pl.BlockSpec(memory_space=pltpu.SMEM)] + [vmem] * 4,
        out_specs=[vmem] * 2,
        name="finish",
    )(core, mine, other, residual, gain)


def shards(memory, kv_weight, mem_lengths, queries, out_weight, residual, norm_gain):
    zh, x, yh, yl, zl, c = (lax.axis_index(a) for a in (Z, X, "yh", "yl", "zl", "c"))
    y = yh * 2 + yl
    where = jnp.stack([zh, x, y]).astype(jnp.int32)

    mine = pick(kv_weight[:, :512], kv_weight[:, 512:], c)
    theirs = pick(kv_weight[:, 512:], kv_weight[:, :512], c)
    rows = pair(mine, swap(theirs, "c"), c)
    rows = pair(rows, swap(rows, "zl"), zl)
    w_mine = lax.all_gather(rows, XY, axis=0, tiled=True)

    step = memory.shape[1] // CHUNKS
    chunks = []
    for j in range(CHUNKS):
        own = memory[:, j * step : (j + 1) * step].reshape(8 * step, 1024)
        prev = lax.ppermute(own, Z, FWD)
        nxt = lax.ppermute(own, Z, BWD)
        chunks.append([own, nxt, prev])
    half = 4 * step
    for chunk in chunks:
        own, nxt, prev = chunk
        opp_a = lax.ppermute(prev[:half], Z, FWD)
        opp_b = lax.ppermute(nxt[half:], Z, BWD)
        chunk[:] = [own, nxt, opp_a, opp_b, prev]

    start = c * 2048 + (x * 4 + y) * 128
    ow = lax.dynamic_slice(out_weight, (zl * 256, start), (256, 128))
    ow = jnp.stack([ow, *ring(ow, Z)])
    other = swap(ow, "zl")
    ow = jnp.where(zl == 0, jnp.concatenate([ow, other], 1), jnp.concatenate([other, ow], 1))
    ow = ow.reshape(2048, 128)

    w_mine, chunks, ow = lax.optimization_barrier((w_mine, chunks, ow))
    ow = lax.all_gather(ow, XY, axis=1, tiled=True)
    w_theirs = swap(w_mine, "c")

    kvs = []
    for pieces in chunks:
        own, oth = project(where, pieces, (w_mine, w_theirs))
        both = pair(own.reshape(8, 1, step, 512), oth.reshape(8, 1, step, 512), c, 1)
        both = lax.all_to_all(both.reshape(16, step, 512), (X, "yh", "c"), 0, 0, tiled=True)
        kvs.append(both.reshape(16 * step, 512))

    queries, _ = lax.optimization_barrier((queries, chunks[-1][2]))
    q = pair(
        pick(queries[:, :DH], queries[:, DH:], c),
        swap(pick(queries[:, DH:], queries[:, :DH], c), "c"),
        c,
    )
    q = pair(q, swap(q, "zl"), zl)
    q = pair(q, swap(q, "yl"), yl)

    length = lax.dynamic_index_in_dim(mem_lengths, x * 2 + yh, 0, keepdims=False)
    here = jnp.stack([length, yl * 256 + zl * 128]).astype(jnp.int32)
    part = attend(here, q, kvs).reshape(2, 2, 2, DH + 16, 256)

    def tokens_of(dy, dz):
        return lax.dynamic_slice(part, (yl ^ dy, zl ^ dz, 0, 0, 0), (1, 1) + part.shape[2:])[0, 0]

    both_swap = [(i, 3 - i) for i in range(4)]
    parts = (
        tokens_of(0, 0),
        swap(tokens_of(1, 0), "yl"),
        swap(tokens_of(0, 1), "zl"),
        lax.ppermute(tokens_of(1, 1), ("yl", "zl"), both_swap),
    )
    head = merge(parts)
    other = swap(pick(head[1], head[0], c), "c")
    mine = pick(head[0], head[1], c)
    context = pair(mine, other, c, 1).reshape(4, 64, 512)

    def section(d):
        return lax.dynamic_index_in_dim(context, (zh + d) % 4, 0, keepdims=False)

    near = [section(0)] + [lax.ppermute(section(4 - d), Z, [(i, (i + 4 - d) % 4) for i in range(4)]) for d in (1, 2, 3)]
    ctx = []
    for a in near:
        ctx += [a, swap(a, "c")]
    mine, theirs = output(where, ctx, ow)
    other = swap(theirs, "c")
    return tuple(finish(c.reshape(1).astype(jnp.int32), mine, other, residual, norm_gain.reshape(1, -1)))


def solution(mesh):
    fine = Mesh(mesh.devices.reshape(4, 4, 2, 2, 2, 2), (Z, X, "yh", "yl", "zl", "c"))
    seq = (X, "yh", "yl", "zl", "c")
    in_specs = (
        P(None, seq, Z),
        P(seq, Z),
        P(),
        P(seq, Z),
        P(Z, None),
        P(seq + (Z,), None),
        P(),
    )
    out_specs = (P(seq + (Z,), None), P(seq + (Z,), None))
    return jax.shard_map(shards, mesh=fine, in_specs=in_specs, out_specs=out_specs, check_vma=False)
```

```python
import functools
import math

import jax
import jax.numpy as jnp
from jax import lax
from jax.experimental import pallas as pl
from jax.experimental.pallas import tpu as pltpu
from jax.sharding import Mesh, PartitionSpec as P


DH = 256
CHUNKS = 2
BF = jnp.bfloat16
F32 = jnp.float32
X = "x"
XY = ("x", "yh", "yl")
Z = "zh"
EXP_SCALE = math.log2(math.e) / math.sqrt(DH)
FWD = [(i, (i + 1) % 4) for i in range(4)]
BWD = [(i, (i + 3) % 4) for i in range(4)]


def swap(a, axis):
    return lax.ppermute(a, axis, [(0, 1), (1, 0)])


def pair(a, b, index, axis=0):
    return jnp.where(index == 0, jnp.concatenate([a, b], axis), jnp.concatenate([b, a], axis))


def pick(a, b, index):
    return jnp.where(index == 0, a, b)


def project_kernel(where_ref, own, nxt, opp_a, opp_b, prev, w_mine, w_theirs, out_ref, buf, sem):
    zh, c = where_ref[0], where_ref[3]
    copies = []
    for dz in range(4):
        block = pl.ds(pl.multiple_of(lax.rem(zh + dz, 4) * 1024, 1024), 1024)
        for j, w in enumerate((w_mine, w_theirs)):
            copies.append(pltpu.make_async_copy(w.at[block], buf.at[2 * dz + j], sem.at[2 * dz + j]))
            copies[-1].start()
    acc = [jnp.zeros((own.shape[0], 2 * DH), F32)] * 2
    for dz in range(4):
        if dz == 2:
            rows = jnp.concatenate([opp_a[...], opp_b[...]], 0)
        else:
            rows = (own, nxt, None, prev)[dz][...]
        for j in range(2):
            copies[2 * dz + j].wait()
            acc[j] = acc[j] + jnp.dot(rows, buf[2 * dz + j], preferred_element_type=F32)
    shape = (out_ref.shape[0],) + out_ref.shape[2:]
    out_ref[:, c] = acc[0].astype(BF).reshape(shape)
    out_ref[:, 1 - c] = acc[1].astype(BF).reshape(shape)


def project(where, pieces, weights):
    rows = pieces[0].shape[0]
    vmem = pl.BlockSpec(memory_space=pltpu.VMEM)
    return pl.pallas_call(
        project_kernel,
        out_shape=jax.ShapeDtypeStruct((8, 2, rows // 8, 2 * DH), BF),
        in_specs=[pl.BlockSpec(memory_space=pltpu.SMEM)] + [vmem] * 5 + [pl.BlockSpec(memory_space=pl.ANY)] * 2,
        out_specs=vmem,
        scratch_shapes=[pltpu.VMEM((8, 1024, 2 * DH), BF), pltpu.SemaphoreType.DMA((8,))],
        name="project",
    )(where, *pieces, *weights)


def attend_kernel(chunk_rows, where_ref, q_ref, *refs):
    kv_refs, out_ref, bias_ref, vt_ref = refs[:-3], refs[-3], refs[-2], refs[-1]
    length, base = where_ref[0], where_ref[1]
    per = chunk_rows // 16

    @pl.when(pl.program_id(0) == 0)
    def _():
        for j in range(len(kv_refs)):
            row = lax.broadcasted_iota(jnp.int32, (chunk_rows, 128), 0)
            source = row // (2 * per)
            side = (row // per) % 2
            position = source * 512 + base + side * 64 + j * per + row % per
            bias_ref[pl.ds(j * chunk_rows, chunk_rows), :] = jnp.where(position < length, 0.0, -1e30)
            vt_ref[j] = kv_refs[j][:, DH:].T

    q = q_ref[...]
    scores = []
    for j, kv in enumerate(kv_refs):
        s = lax.dot_general(kv[:, :DH], q, (((1,), (1,)), ((), ())), preferred_element_type=F32)
        bias = bias_ref[pl.ds(j * chunk_rows, chunk_rows), :]
        scores.append(s + jnp.concatenate([bias] * (q.shape[0] // 128), axis=1))
    high = functools.reduce(jnp.maximum, [jnp.max(s, axis=0, keepdims=True) for s in scores])
    total = jnp.zeros_like(high)
    acc = jnp.zeros((DH, q.shape[0]), F32)
    for j, s in enumerate(scores):
        p = jnp.exp2((s - high) * EXP_SCALE)
        total += jnp.sum(p, axis=0, keepdims=True)
        acc += jnp.dot(vt_ref[j], p.astype(BF), preferred_element_type=F32)
    out_ref[0, :DH] = (acc / total).astype(BF)
    lse = high * EXP_SCALE + jnp.log2(total)
    first = lse.astype(BF)
    rest = lse - first.astype(F32)
    second = rest.astype(BF)
    third = (rest - second.astype(F32)).astype(BF)
    zero = jnp.zeros((13, q.shape[0]), F32)
    stats = jnp.concatenate([first.astype(F32), second.astype(F32), third.astype(F32), zero], 0)
    out_ref[0, DH:] = stats.astype(BF)


def attend(where, q, kvs):
    rows = kvs[0].shape[0]
    tokens = q.shape[0]
    whole = pl.BlockSpec((rows, 2 * DH), lambda i: (0, 0))
    return pl.pallas_call(
        functools.partial(attend_kernel, rows),
        grid=(tokens // 256,),
        out_shape=jax.ShapeDtypeStruct((tokens // 256, DH + 16, 256), BF),
        in_specs=[pl.BlockSpec(memory_space=pltpu.SMEM), pl.BlockSpec((256, DH), lambda i: (i, 0))] + [whole] * len(kvs),
        out_specs=pl.BlockSpec((1, DH + 16, 256), lambda i: (i, 0, 0)),
        scratch_shapes=[pltpu.VMEM((rows * len(kvs), 128), F32), pltpu.VMEM((len(kvs), DH, rows), BF)],
        name="attend",
    )(where, q, *kvs)


def merge_kernel(a_ref, b_ref, c_ref, d_ref, out_ref):
    refs = (a_ref, b_ref, c_ref, d_ref)
    for side in range(2):
        stats = [ref[side, DH:].astype(F32) for ref in refs]
        lse = [s[0:1] + s[1:2] + s[2:3] for s in stats]
        high = functools.reduce(jnp.maximum, lse)
        weight = [jnp.exp2(v - high) for v in lse]
        inverse = 1.0 / sum(weight)
        context = sum(ref[side, :DH].astype(F32) * (w * inverse) for ref, w in zip(refs, weight))
        out_ref[side] = context.T.astype(BF)


def merge(parts):
    vmem = pl.BlockSpec(memory_space=pltpu.VMEM)
    return pl.pallas_call(
        merge_kernel,
        out_shape=jax.ShapeDtypeStruct((2, 256, DH), BF),
        in_specs=[vmem] * 4,
        out_specs=vmem,
        name="merge",
    )(*parts)


def output_kernel(where_ref, *refs):
    ctx, w_ref, out_own, out_oth, acc = refs[:8], refs[8], refs[9], refs[10], refs[11]
    k = pl.program_id(0)

    @pl.when(k == 0)
    def _():
        acc[...] = jnp.zeros_like(acc)

    rows = jnp.concatenate([ctx[0][...], ctx[1][...]], 0)
    for dz in range(1, 4):
        rows = jnp.where(k == dz, jnp.concatenate([ctx[2 * dz][...], ctx[2 * dz + 1][...]], 0), rows)
    acc[...] += jnp.dot(rows, w_ref[...], preferred_element_type=F32)

    @pl.when(k == 3)
    def _():
        out_own[...] = acc[:64]
        out_oth[...] = acc[64:]


def output(where, ctx, w):
    whole = pl.BlockSpec((64, 2 * DH), lambda i: (0, 0))
    out = pl.BlockSpec((64, 2048), lambda i: (0, 0))
    return pl.pallas_call(
        output_kernel,
        grid=(4,),
        out_shape=[jax.ShapeDtypeStruct((64, 2048), F32)] * 2,
        in_specs=[pl.BlockSpec(memory_space=pltpu.SMEM)] + [whole] * 8 + [pl.BlockSpec((512, 2048), lambda i: (i, 0))],
        out_specs=[out] * 2,
        scratch_shapes=[pltpu.VMEM((128, 2048), F32)],
        name="output",
    )(where, *ctx, w)


def finish_kernel(c_ref, mine, other, residual, gain, hidden, normed):
    swapped = c_ref[0] == 1
    a, b = mine[...], other[...]
    low = residual[:, :2048].astype(F32) + jnp.where(swapped, b, a)
    high = residual[:, 2048:].astype(F32) + jnp.where(swapped, a, b)
    squares = jnp.sum(low * low, -1, keepdims=True) + jnp.sum(high * high, -1, keepdims=True)
    scale = lax.rsqrt(squares * (1.0 / 4096) + 1e-06)
    hidden[:, :2048] = low.astype(BF)
    hidden[:, 2048:] = high.astype(BF)
    normed[:, :2048] = (low * scale * gain[:, :2048]).astype(BF)
    normed[:, 2048:] = (high * scale * gain[:, 2048:]).astype(BF)


def finish(core, mine, other, residual, gain):
    vmem = pl.BlockSpec(memory_space=pltpu.VMEM)
    return pl.pallas_call(
        finish_kernel,
        out_shape=[jax.ShapeDtypeStruct(residual.shape, BF)] * 2,
        in_specs=[pl.BlockSpec(memory_space=pltpu.SMEM)] + [vmem] * 4,
        out_specs=[vmem] * 2,
        name="finish",
    )(core, mine, other, residual, gain)


def shards(memory, kv_weight, mem_lengths, queries, out_weight, residual, norm_gain):
    zh, x, yh, yl, zl, c = (lax.axis_index(a) for a in (Z, X, "yh", "yl", "zl", "c"))
    y = yh * 2 + yl
    where = jnp.stack([zh, x, y, c]).astype(jnp.int32)

    mine = pick(kv_weight[:, :512], kv_weight[:, 512:], c)
    theirs = pick(kv_weight[:, 512:], kv_weight[:, :512], c)
    w_c = swap(theirs, "c")
    w_z = swap(mine, "zl")
    w_zc = lax.ppermute(theirs, ("zl", "c"), [(i, 3 - i) for i in range(4)])
    rows = pair(pair(mine, w_c, c), pair(w_z, w_zc, c), zl)
    w_mine = lax.all_gather(rows, XY, axis=0, tiled=True)

    step = memory.shape[1] // CHUNKS
    half = 4 * step
    chunks = []
    for j in range(CHUNKS):
        own = memory[:, j * step : (j + 1) * step].reshape(8 * step, 1024)
        prev = lax.ppermute(own, Z, FWD)
        nxt = lax.ppermute(own, Z, BWD)
        opp_a = lax.ppermute(prev[:half], Z, FWD)
        opp_b = lax.ppermute(nxt[half:], Z, BWD)
        chunks.append([own, nxt, opp_a, opp_b, prev])

    ow = lax.dynamic_slice(out_weight, (0, c * 2048 + (x * 4 + y) * 128), (512, 128))
    ow = [ow] + [lax.ppermute(ow, Z, [(i, (i + 4 - d) % 4) for i in range(4)]) for d in (1, 2, 3)]
    ow = jnp.concatenate(ow, 0)

    w_mine, ow = lax.optimization_barrier((w_mine, ow))
    ow = lax.all_gather(ow, XY, axis=1, tiled=True)
    w_theirs = swap(w_mine, "c")

    kvs = []
    for pieces in chunks:
        both = project(where, pieces, (w_mine, w_theirs))
        both = lax.all_to_all(both.reshape(16, step, 512), (X, "yh", "c"), 0, 0, tiled=True)
        kvs.append(both.reshape(16 * step, 512))

    other = pick(queries[:, DH:], queries[:, :DH], c)
    other = swap(other, "c")
    q = pair(pick(queries[:, :DH], queries[:, DH:], c), other, c)
    q = pair(q, swap(q, "zl"), zl)
    q = pair(q, swap(q, "yl"), yl)

    length = lax.dynamic_index_in_dim(mem_lengths, x * 2 + yh, 0, keepdims=False)
    here = jnp.stack([length, yl * 256 + zl * 128]).astype(jnp.int32)
    part = attend(here, q, kvs).reshape(2, 2, 2, DH + 16, 256)

    def tokens_of(dy, dz):
        return lax.dynamic_slice(part, (yl ^ dy, zl ^ dz, 0, 0, 0), (1, 1) + part.shape[2:])[0, 0]

    both_swap = [(i, 3 - i) for i in range(4)]
    parts = (
        tokens_of(0, 0),
        swap(tokens_of(1, 0), "yl"),
        swap(tokens_of(0, 1), "zl"),
        lax.ppermute(tokens_of(1, 1), ("yl", "zl"), both_swap),
    )
    head = merge(parts)
    other = swap(pick(head[1], head[0], c), "c")
    mine = pick(head[0], head[1], c)
    context = pair(mine, other, c, 1).reshape(4, 64, 512)

    def section(d):
        return lax.dynamic_index_in_dim(context, (zh + d) % 4, 0, keepdims=False)

    near = [section(0)] + [lax.ppermute(section(4 - d), Z, [(i, (i + 4 - d) % 4) for i in range(4)]) for d in (1, 2, 3)]
    ctx = []
    for a in near:
        ctx += [a, swap(a, "c")]
    mine, theirs = output(where, ctx, ow)
    other = swap(theirs, "c")
    return tuple(finish(c.reshape(1).astype(jnp.int32), mine, other, residual, norm_gain.reshape(1, -1)))


def solution(mesh):
    fine = Mesh(mesh.devices.reshape(4, 4, 2, 2, 2, 2), (Z, X, "yh", "yl", "zl", "c"))
    seq = (X, "yh", "yl", "zl", "c")
    in_specs = (
        P(None, seq, Z),
        P(seq, Z),
        P(),
        P(seq, Z),
        P(Z, None),
        P(seq + (Z,), None),
        P(),
    )
    out_specs = (P(seq + (Z,), None), P(seq + (Z,), None))
    return jax.shard_map(shards, mesh=fine, in_specs=in_specs, out_specs=out_specs, check_vma=False)
```

```python
import functools
import math

import jax
import jax.numpy as jnp
from jax import lax
from jax.experimental import pallas as pl
from jax.experimental.pallas import tpu as pltpu
from jax.sharding import Mesh, PartitionSpec as P


DH = 256
CHUNKS = 2
BF = jnp.bfloat16
F32 = jnp.float32
X = "x"
XY = ("x", "yh", "yl")
Z = "zh"
EXP_SCALE = math.log2(math.e) / math.sqrt(DH)
FWD = [(i, (i + 1) % 4) for i in range(4)]
BWD = [(i, (i + 3) % 4) for i in range(4)]


def swap(a, axis):
    return lax.ppermute(a, axis, [(0, 1), (1, 0)])


def pair(a, b, index, axis=0):
    return jnp.where(index == 0, jnp.concatenate([a, b], axis), jnp.concatenate([b, a], axis))


def pick(a, b, index):
    return jnp.where(index == 0, a, b)


def project_kernel(where_ref, own, nxt, opp_a, opp_b, prev, w_mine, w_theirs, out_ref, buf, sem):
    zh, c = where_ref[0], where_ref[3]
    copies = []
    for dz in range(4):
        block = pl.ds(pl.multiple_of(lax.rem(zh + dz, 4) * 1024, 1024), 1024)
        for j, w in enumerate((w_mine, w_theirs)):
            copies.append(pltpu.make_async_copy(w.at[block], buf.at[2 * dz + j], sem.at[2 * dz + j]))
            copies[-1].start()
    acc = [jnp.zeros((own.shape[0], 2 * DH), F32)] * 2
    for dz in range(4):
        if dz == 2:
            rows = jnp.concatenate([opp_a[...], opp_b[...]], 0)
        else:
            rows = (own, nxt, None, prev)[dz][...]
        for j in range(2):
            copies[2 * dz + j].wait()
            acc[j] = acc[j] + jnp.dot(rows, buf[2 * dz + j], preferred_element_type=F32)
    shape = (out_ref.shape[0],) + out_ref.shape[2:]
    out_ref[:, c] = acc[0].astype(BF).reshape(shape)
    out_ref[:, 1 - c] = acc[1].astype(BF).reshape(shape)


def project(where, pieces, weights):
    rows = pieces[0].shape[0]
    vmem = pl.BlockSpec(memory_space=pltpu.VMEM)
    return pl.pallas_call(
        project_kernel,
        out_shape=jax.ShapeDtypeStruct((8, 2, rows // 8, 2 * DH), BF),
        in_specs=[pl.BlockSpec(memory_space=pltpu.SMEM)] + [vmem] * 5 + [pl.BlockSpec(memory_space=pl.ANY)] * 2,
        out_specs=vmem,
        scratch_shapes=[pltpu.VMEM((8, 1024, 2 * DH), BF), pltpu.SemaphoreType.DMA((8,))],
        name="project",
    )(where, *pieces, *weights)


def attend_kernel(chunk, last, where_ref, q_ref, kv_ref, *refs):
    length, base = where_ref[0], where_ref[1]
    step = pl.program_id(0)
    rows = kv_ref.shape[0]
    per = rows // 16
    bias_ref, vt_ref = refs[-2:]
    if last:
        acc_in, stats_in, outs = refs[0], refs[1], refs[2:6]
    else:
        acc_out, stats_out = refs[0], refs[1]

    @pl.when(step == 0)
    def _():
        row = lax.broadcasted_iota(jnp.int32, (rows, 128), 0)
        source = row // (2 * per)
        side = (row // per) % 2
        position = source * 512 + base + side * 64 + chunk * per + row % per
        bias_ref[...] = jnp.where(position < length, 0.0, -1e30)
        vt_ref[...] = kv_ref[:, DH:].T

    q = q_ref[...]
    s = lax.dot_general(kv_ref[:, :DH], q, (((1,), (1,)), ((), ())), preferred_element_type=F32)
    bias = bias_ref[...]
    s = s + jnp.concatenate([bias, bias], axis=1)
    high = jnp.max(s, axis=0, keepdims=True)
    if last:
        before = stats_in[0, 0:1]
        high = jnp.maximum(high, before)
    p = jnp.exp2((s - high) * EXP_SCALE)
    total = jnp.sum(p, axis=0, keepdims=True)
    acc = jnp.dot(vt_ref[...], p.astype(BF), preferred_element_type=F32)
    if not last:
        acc_out[0] = acc
        stats_out[0] = jnp.concatenate([high, total, jnp.zeros((6, 256), F32)], 0)
        return
    keep = jnp.exp2((before - high) * EXP_SCALE)
    total = total + stats_in[0, 1:2] * keep
    acc = acc + acc_in[0] * keep
    context = (acc * (1.0 / total)).astype(BF)
    lse = high * EXP_SCALE + jnp.log2(total)
    first = lse.astype(BF).astype(F32)
    second = (lse - first).astype(BF).astype(F32)
    third = lse - first - second
    stats = jnp.concatenate([first, second, third, jnp.zeros((13, 256), F32)], 0).astype(BF)
    for r, out in enumerate(outs):

        @pl.when(step // 2 == r)
        def _(out=out):
            out[0, :DH] = context
            out[0, DH:] = stats


def attend(where, q, kv, chunk, before=None):
    last = before is not None
    rows = kv.shape[0]

    def block(i, where):
        return where[2 + i // 2] * 2 + i % 2

    state = [pl.BlockSpec((1, DH, 256), lambda i, w: (i, 0, 0)), pl.BlockSpec((1, 8, 256), lambda i, w: (i, 0, 0))]
    if last:
        outs = [jax.ShapeDtypeStruct((2, DH + 16, 256), BF)] * 4
        out_specs = [
            pl.BlockSpec((1, DH + 16, 256), lambda i, w, r=r: (jnp.clip(i - 2 * r, 0, 1), 0, 0)) for r in range(4)
        ]
    else:
        outs = [jax.ShapeDtypeStruct((8, DH, 256), F32), jax.ShapeDtypeStruct((8, 8, 256), F32)]
        out_specs = state
    return pl.pallas_call(
        functools.partial(attend_kernel, chunk, last),
        out_shape=outs,
        grid_spec=pltpu.PrefetchScalarGridSpec(
            num_scalar_prefetch=1,
            grid=(8,),
            in_specs=[
                pl.BlockSpec((256, DH), lambda i, w: (block(i, w), 0)),
                pl.BlockSpec((rows, 2 * DH), lambda i, w: (0, 0)),
            ]
            + (state if last else []),
            out_specs=out_specs,
            scratch_shapes=[pltpu.VMEM((rows, 128), F32), pltpu.VMEM((DH, rows), BF)],
        ),
        name="attend",
    )(where, q, kv, *(before or ()))


def merge_kernel(where_ref, a_ref, b_ref, c_ref, d_ref, *outs):
    zh = where_ref[0]
    refs = (a_ref, b_ref, c_ref, d_ref)
    contexts = []
    for side in range(2):
        stats = [ref[side, DH:].astype(F32) for ref in refs]
        lse = [s[0:1] + s[1:2] + s[2:3] for s in stats]
        high = functools.reduce(jnp.maximum, lse)
        weight = [jnp.exp2(v - high) for v in lse]
        inverse = 1.0 / sum(weight)
        context = sum(ref[side, :DH].astype(F32) * (w * inverse) for ref, w in zip(refs, weight))
        contexts.append(context.T.astype(BF))
    for d in range(4):
        for m in range(4):

            @pl.when(lax.rem(zh + d, 4) == m)
            def _(d=d, m=m):
                for side in range(2):
                    outs[d][side * 64 : (side + 1) * 64] = contexts[side][m * 64 : (m + 1) * 64]


def merge(where, parts):
    vmem = pl.BlockSpec(memory_space=pltpu.VMEM)
    return pl.pallas_call(
        merge_kernel,
        out_shape=[jax.ShapeDtypeStruct((128, DH), BF)] * 4,
        in_specs=[pl.BlockSpec(memory_space=pltpu.SMEM)] + [vmem] * 4,
        out_specs=[vmem] * 4,
        name="merge",
    )(where, *parts)


def output_kernel(where_ref, *refs):
    c = where_ref[3]
    w_ref, out_mine, out_theirs = refs[4:]
    rows = jnp.concatenate([ref[...] for ref in refs[:4]], 1)
    acc = jnp.dot(rows, w_ref[...], preferred_element_type=F32)
    low, high = acc[:64], acc[64:]
    out_mine[...] = jnp.where(c == 0, low, high)
    out_theirs[...] = jnp.where(c == 0, high, low)


def output(where, ctx, w):
    whole = pl.BlockSpec((128, DH), lambda i: (0, 0))
    out = pl.BlockSpec((64, 512), lambda i: (0, i))
    return pl.pallas_call(
        output_kernel,
        grid=(8,),
        out_shape=[jax.ShapeDtypeStruct((64, 4096), F32)] * 2,
        in_specs=[pl.BlockSpec(memory_space=pltpu.SMEM)] + [whole] * 4 + [pl.BlockSpec((1024, 512), lambda i: (0, i))],
        out_specs=[out] * 2,
        name="output",
    )(where, *ctx, w)


def finish_kernel(mine, other, residual, gain, hidden, normed):
    x = residual[...].astype(F32) + (mine[...] + other[...])
    scale = lax.rsqrt(jnp.mean(x * x, -1, keepdims=True) + 1e-06)
    hidden[...] = x.astype(BF)
    normed[...] = (x * scale * gain[...]).astype(BF)


def finish(mine, other, residual, gain):
    rows = pl.BlockSpec((16, 4096), lambda i: (i, 0))
    return pl.pallas_call(
        finish_kernel,
        grid=(4,),
        out_shape=[jax.ShapeDtypeStruct(residual.shape, BF)] * 2,
        in_specs=[rows] * 3 + [pl.BlockSpec((1, 4096), lambda i: (0, 0))],
        out_specs=[rows] * 2,
        name="finish",
    )(mine, other, residual, gain)


def shards(memory, kv_weight, mem_lengths, queries, out_weight, residual, norm_gain):
    zh, x, yh, yl, zl, c = (lax.axis_index(a) for a in (Z, X, "yh", "yl", "zl", "c"))
    y = yh * 2 + yl
    where = jnp.stack([zh, x, y, c]).astype(jnp.int32)

    mine = pick(kv_weight[:, :512], kv_weight[:, 512:], c)
    theirs = pick(kv_weight[:, 512:], kv_weight[:, :512], c)
    w_c = swap(theirs, "c")
    w_z = swap(mine, "zl")
    w_zc = lax.ppermute(theirs, ("zl", "c"), [(i, 3 - i) for i in range(4)])
    rows = pair(pair(mine, w_c, c), pair(w_z, w_zc, c), zl)
    w_mine = lax.all_gather(rows, XY, axis=0, tiled=True)

    step = memory.shape[1] // CHUNKS
    half = 4 * step
    chunks = []
    for j in range(CHUNKS):
        own = memory[:, j * step : (j + 1) * step].reshape(8 * step, 1024)
        prev = lax.ppermute(own, Z, FWD)
        nxt = lax.ppermute(own, Z, BWD)
        opp_a = lax.ppermute(prev[:half], Z, FWD)
        opp_b = lax.ppermute(nxt[half:], Z, BWD)
        chunks.append([own, nxt, opp_a, opp_b, prev])

    ow = lax.dynamic_slice(out_weight, (c * DH, (x * 4 + y) * 256), (DH, 256))
    ow = [ow] + [lax.ppermute(ow, Z, [(i, (i + 4 - d) % 4) for i in range(4)]) for d in (1, 2, 3)]
    ow = jnp.concatenate(ow, 0)

    w_mine, ow = lax.optimization_barrier((w_mine, ow))
    ow = lax.all_gather(ow, XY, axis=1, tiled=True)
    w_theirs = swap(w_mine, "c")

    other = pick(queries[:, DH:], queries[:, :DH], c)
    other = swap(other, "c")
    q = pair(pick(queries[:, :DH], queries[:, DH:], c), other, c)
    q = pair(q, swap(q, "zl"), zl)
    q = pair(q, swap(q, "yl"), yl)

    length = lax.dynamic_index_in_dim(mem_lengths, x * 2 + yh, 0, keepdims=False)
    here = yl * 2 + zl
    here = jnp.stack([length, yl * 256 + zl * 128, here, here ^ 1, here ^ 2, here ^ 3]).astype(jnp.int32)
    state = None
    for j, pieces in enumerate(chunks):
        both = project(where, pieces, (w_mine, w_theirs))
        both = lax.all_to_all(both.reshape(16, step, 512), (X, "yh", "c"), 0, 0, tiled=True)
        state = attend(here, q, both.reshape(16 * step, 512), j, state)

    own, to_zl, to_yl, to_both = state
    parts = (
        own,
        swap(to_zl, "zl"),
        swap(to_yl, "yl"),
        lax.ppermute(to_both, ("yl", "zl"), [(i, 3 - i) for i in range(4)]),
    )
    pieces = merge(where, parts)
    ctx = [pieces[0]] + [lax.ppermute(pieces[4 - d], Z, [(i, (i + 4 - d) % 4) for i in range(4)]) for d in (1, 2, 3)]
    mine, theirs = output(where, ctx, ow)
    return tuple(finish(mine, swap(theirs, "c"), residual, norm_gain.reshape(1, -1)))


def solution(mesh):
    fine = Mesh(mesh.devices.reshape(4, 4, 2, 2, 2, 2), (Z, X, "yh", "yl", "zl", "c"))
    seq = (X, "yh", "yl", "zl", "c")
    in_specs = (
        P(None, seq, Z),
        P(seq, Z),
        P(),
        P(seq, Z),
        P(Z, None),
        P(seq + (Z,), None),
        P(),
    )
    out_specs = (P(seq + (Z,), None), P(seq + (Z,), None))
    return jax.shard_map(shards, mesh=fine, in_specs=in_specs, out_specs=out_specs, check_vma=False)
```

```python
import functools
import math

import jax
import jax.numpy as jnp
from jax import lax
from jax.experimental import pallas as pl
from jax.experimental.pallas import tpu as pltpu
from jax.sharding import Mesh, PartitionSpec as P


DH = 256
CHUNKS = 2
VMEM_LIMIT = 16 << 20
BF = jnp.bfloat16
F32 = jnp.float32
X = "x"
XY = ("x", "yh", "yl")
Z = "zh"
EXP_SCALE = math.log2(math.e) / math.sqrt(DH)
FWD = [(i, (i + 1) % 4) for i in range(4)]
BWD = [(i, (i + 3) % 4) for i in range(4)]


def swap(a, axis):
    return lax.ppermute(a, axis, [(0, 1), (1, 0)])


def pair(a, b, index, axis=0):
    return jnp.where(index == 0, jnp.concatenate([a, b], axis), jnp.concatenate([b, a], axis))


def pick(a, b, index):
    return jnp.where(index == 0, a, b)


def kernel_call(kernel, outs, where, *args):
    spec = pl.BlockSpec(memory_space=pltpu.VMEM)
    args = [pltpu.with_memory_space_constraint(a, pltpu.VMEM) for a in args]
    return pl.pallas_call(
        kernel,
        out_shape=outs,
        in_specs=[pl.BlockSpec(memory_space=pltpu.SMEM)] + [spec] * len(args),
        out_specs=[spec] * len(outs),
        compiler_params=pltpu.CompilerParams(vmem_limit_bytes=VMEM_LIMIT),
    )(where, *args)


def project_kernel(where_ref, own, nxt, opp_a, opp_b, prev, w_mine, w_theirs, out_ref):
    zh, c = where_ref[0], where_ref[3]
    acc = [jnp.zeros((own.shape[0], 2 * DH), F32)] * 2
    for dz in range(4):
        block = pl.ds(pl.multiple_of(lax.rem(zh + dz, 4) * 1024, 1024), 1024)
        if dz == 2:
            rows = jnp.concatenate([opp_a[...], opp_b[...]], 0)
        else:
            rows = (own, nxt, None, prev)[dz][...]
        for j, w in enumerate((w_mine, w_theirs)):
            acc[j] = acc[j] + jnp.dot(rows, w[block], preferred_element_type=F32)
    shape = (out_ref.shape[0],) + out_ref.shape[2:]
    out_ref[:, c] = acc[0].astype(BF).reshape(shape)
    out_ref[:, 1 - c] = acc[1].astype(BF).reshape(shape)


def project(where, pieces, weights):
    out = jax.ShapeDtypeStruct((8, 2, pieces[0].shape[0] // 8, 2 * DH), BF)
    return kernel_call(project_kernel, [out], where, *pieces, *weights)[0]


def attend_kernel(chunk, last, where_ref, q_ref, kv_ref, *refs):
    length, base = where_ref[0], where_ref[1]
    rows = kv_ref.shape[0]
    per = rows // 16
    if last:
        acc_in, stats_in, outs = refs[0], refs[1], refs[2:]
    else:
        acc_out, stats_out = refs
    row = lax.broadcasted_iota(jnp.int32, (rows, 128), 0)
    shift = per.bit_length() - 1
    position = (row >> (shift + 1)) * 512 + base + ((row >> shift) & 1) * 64 + chunk * per + (row & (per - 1))
    bias = jnp.where(position < length, 0.0, -1e30)
    bias = jnp.concatenate([bias, bias], axis=1)
    keys = kv_ref[:, :DH]
    values = kv_ref[:, DH:].T
    for i in range(8):
        group = where_ref[2 + i // 2] * 2 + i % 2
        q = q_ref[pl.ds(pl.multiple_of(group * 256, 256), 256)]
        s = lax.dot_general(keys, q, (((1,), (1,)), ((), ())), preferred_element_type=F32) + bias
        high = jnp.max(s, axis=0, keepdims=True)
        if last:
            before = stats_in[i, 0:1]
            high = jnp.maximum(high, before)
        p = jnp.exp2((s - high) * EXP_SCALE)
        total = jnp.sum(p, axis=0, keepdims=True)
        acc = jnp.dot(values, p.astype(BF), preferred_element_type=F32)
        if not last:
            acc_out[i] = acc
            stats_out[i] = jnp.concatenate([high, total, jnp.zeros((6, 256), F32)], 0)
            continue
        keep = jnp.exp2((before - high) * EXP_SCALE)
        total = total + stats_in[i, 1:2] * keep
        acc = acc + acc_in[i] * keep
        lse = high * EXP_SCALE + jnp.log2(total)
        first = lse.astype(BF).astype(F32)
        second = (lse - first).astype(BF).astype(F32)
        stats = jnp.concatenate([first, second, lse - first - second, jnp.zeros((13, 256), F32)], 0)
        outs[i // 2][i % 2, :DH] = (acc * (1.0 / total)).astype(BF)
        outs[i // 2][i % 2, DH:] = stats.astype(BF)


def attend(where, q, kv, chunk, before=None):
    last = before is not None
    if last:
        outs = [jax.ShapeDtypeStruct((2, DH + 16, 256), BF)] * 4
    else:
        outs = [jax.ShapeDtypeStruct((8, DH, 256), F32), jax.ShapeDtypeStruct((8, 8, 256), F32)]
    kernel = functools.partial(attend_kernel, chunk, last)
    return kernel_call(kernel, outs, where, q, kv, *(before or ()))


def merge_kernel(where_ref, a_ref, b_ref, c_ref, d_ref, *outs):
    zh = where_ref[0]
    refs = (a_ref, b_ref, c_ref, d_ref)
    contexts = []
    for side in range(2):
        stats = [ref[side, DH:].astype(F32) for ref in refs]
        lse = [s[0:1] + s[1:2] + s[2:3] for s in stats]
        high = functools.reduce(jnp.maximum, lse)
        weight = [jnp.exp2(v - high) for v in lse]
        inverse = 1.0 / sum(weight)
        context = sum(ref[side, :DH].astype(F32) * (w * inverse) for ref, w in zip(refs, weight))
        contexts.append(context.T.astype(BF))
    for d in range(4):
        for m in range(4):

            @pl.when(lax.rem(zh + d, 4) == m)
            def _(d=d, m=m):
                for side in range(2):
                    outs[d][side * 64 : (side + 1) * 64] = contexts[side][m * 64 : (m + 1) * 64]


def merge(where, parts):
    return kernel_call(merge_kernel, [jax.ShapeDtypeStruct((128, DH), BF)] * 4, where, *parts)


def output_kernel(where_ref, *refs):
    c = where_ref[3]
    w_ref, out_mine, out_theirs = refs[4:]
    rows = jnp.concatenate([ref[...] for ref in refs[:4]], 1)
    for i in range(8):
        cols = slice(i * 512, (i + 1) * 512)
        acc = jnp.dot(rows, w_ref[:, cols], preferred_element_type=F32)
        low, high = acc[:64], acc[64:]
        out_mine[:, cols] = jnp.where(c == 0, low, high)
        out_theirs[:, cols] = jnp.where(c == 0, high, low)


def output(where, ctx, w):
    return kernel_call(output_kernel, [jax.ShapeDtypeStruct((64, 4096), F32)] * 2, where, *ctx, w)


def finish_kernel(where_ref, mine, other, residual, gain, hidden, normed):
    x = residual[...].astype(F32) + (mine[...] + other[...])
    scale = lax.rsqrt(jnp.mean(x * x, -1, keepdims=True) + 1e-06)
    hidden[...] = x.astype(BF)
    normed[...] = (x * scale * gain[...]).astype(BF)


def finish(where, *args):
    return kernel_call(finish_kernel, [jax.ShapeDtypeStruct(args[2].shape, BF)] * 2, where, *args)


def shards(memory, kv_weight, mem_lengths, queries, out_weight, residual, norm_gain):
    zh, x, yh, yl, zl, c = (lax.axis_index(a) for a in (Z, X, "yh", "yl", "zl", "c"))
    y = yh * 2 + yl
    where = jnp.stack([zh, x, y, c]).astype(jnp.int32)

    mine = pick(kv_weight[:, :512], kv_weight[:, 512:], c)
    theirs = pick(kv_weight[:, 512:], kv_weight[:, :512], c)
    w_c = swap(theirs, "c")
    w_z = swap(mine, "zl")
    w_zc = lax.ppermute(theirs, ("zl", "c"), [(i, 3 - i) for i in range(4)])
    rows = pair(pair(mine, w_c, c), pair(w_z, w_zc, c), zl)
    w_mine = lax.all_gather(rows, XY, axis=0, tiled=True)

    step = memory.shape[1] // CHUNKS
    half = 4 * step
    chunks = []
    for j in range(CHUNKS):
        own = memory[:, j * step : (j + 1) * step].reshape(8 * step, 1024)
        prev = lax.ppermute(own, Z, FWD)
        nxt = lax.ppermute(own, Z, BWD)
        opp_a = lax.ppermute(prev[:half], Z, FWD)
        opp_b = lax.ppermute(nxt[half:], Z, BWD)
        chunks.append([own, nxt, opp_a, opp_b, prev])

    ow = lax.dynamic_slice(out_weight, (c * DH, (x * 4 + y) * 256), (DH, 256))
    ow = [ow] + [lax.ppermute(ow, Z, [(i, (i + 4 - d) % 4) for i in range(4)]) for d in (1, 2, 3)]
    ow = jnp.concatenate(ow, 0)

    w_mine, ow = lax.optimization_barrier((w_mine, ow))
    ow = lax.all_gather(ow, XY, axis=1, tiled=True)
    w_theirs = swap(w_mine, "c")

    other = pick(queries[:, DH:], queries[:, :DH], c)
    other = swap(other, "c")
    q = pair(pick(queries[:, :DH], queries[:, DH:], c), other, c)
    other = swap(q, "zl")
    q = pair(q, other, zl)
    q = pair(q, swap(q, "yl"), yl)

    length = lax.dynamic_index_in_dim(mem_lengths, x * 2 + yh, 0, keepdims=False)
    here = yl * 2 + zl
    here = jnp.stack([length, yl * 256 + zl * 128, here, here ^ 1, here ^ 2, here ^ 3]).astype(jnp.int32)
    state = None
    for j, pieces in enumerate(chunks):
        both = project(where, pieces, (w_mine, w_theirs))
        both = lax.all_to_all(both.reshape(16, step, 512), (X, "yh", "c"), 0, 0, tiled=True)
        state = attend(here, q, both.reshape(16 * step, 512), j, state)

    own, to_zl, to_yl, to_both = state
    parts = (
        own,
        swap(to_zl, "zl"),
        swap(to_yl, "yl"),
        lax.ppermute(to_both, ("yl", "zl"), [(i, 3 - i) for i in range(4)]),
    )
    pieces = merge(where, parts)
    ctx = [pieces[0]] + [lax.ppermute(pieces[4 - d], Z, [(i, (i + 4 - d) % 4) for i in range(4)]) for d in (1, 2, 3)]
    mine, theirs = output(where, ctx, ow)
    return tuple(finish(where, mine, swap(theirs, "c"), residual, norm_gain.reshape(1, -1)))


def solution(mesh):
    fine = Mesh(mesh.devices.reshape(4, 4, 2, 2, 2, 2), (Z, X, "yh", "yl", "zl", "c"))
    seq = (X, "yh", "yl", "zl", "c")
    in_specs = (
        P(None, seq, Z),
        P(seq, Z),
        P(),
        P(seq, Z),
        P(Z, None),
        P(seq + (Z,), None),
        P(),
    )
    out_specs = (P(seq + (Z,), None), P(seq + (Z,), None))
    return jax.shard_map(shards, mesh=fine, in_specs=in_specs, out_specs=out_specs, check_vma=False)
```

```python
import functools
import math

import jax
import jax.numpy as jnp
from jax import lax
from jax.experimental import pallas as pl
from jax.experimental.pallas import tpu as pltpu
from jax.sharding import Mesh, PartitionSpec as P


DH = 256
CHUNKS = 2
VMEM_LIMIT = 16 << 20
BF = jnp.bfloat16
F32 = jnp.float32
X = "x"
Y = ("yh", "yl")
XY = ("x", "yh", "yl")
Z = "zh"
EXP_SCALE = math.log2(math.e) / math.sqrt(DH)
FWD = [(i, (i + 1) % 4) for i in range(4)]
BWD = [(i, (i + 3) % 4) for i in range(4)]


def swap(a, axis):
    return lax.ppermute(a, axis, [(0, 1), (1, 0)])


def beyond(a, axis):
    return [lax.ppermute(a, axis, [(i, (i + 4 - d) % 4) for i in range(4)]) for d in (1, 2, 3)]


def pair(a, b, index, axis=0):
    return jnp.where(index == 0, jnp.concatenate([a, b], axis), jnp.concatenate([b, a], axis))


def pick(a, b, index):
    return jnp.where(index == 0, a, b)


def kernel_call(kernel, outs, where, *args):
    spec = pl.BlockSpec(memory_space=pltpu.VMEM)
    args = [pltpu.with_memory_space_constraint(a, pltpu.VMEM) for a in args]
    return pl.pallas_call(
        kernel,
        out_shape=outs,
        in_specs=[pl.BlockSpec(memory_space=pltpu.SMEM)] + [spec] * len(args),
        out_specs=[spec] * len(outs),
        compiler_params=pltpu.CompilerParams(vmem_limit_bytes=VMEM_LIMIT),
    )(where, *args)


def project_kernel(where_ref, own, nxt, opp_a, opp_b, prev, wk_mine, wv_mine, wk_theirs, wv_theirs, out_ref):
    zh, x, y, c = where_ref[0], where_ref[1], where_ref[2], where_ref[3]
    acc = [jnp.zeros((own.shape[0], DH), F32)] * 4
    for dz in range(4):
        dx = lax.rem(zh + dz + 4 - x, 4)
        if dz == 2:
            rows = jnp.concatenate([opp_a[...], opp_b[...]], 0)
        else:
            rows = (own, nxt, None, prev)[dz][...]
        for j, w in enumerate((wk_mine, wv_mine, wk_theirs, wv_theirs)):
            near = [lax.rem(i + 4 - y, 4) for i in range(4)]
            blocks = [w[dy, dx] if j % 2 == 0 else w[dx, dy] for dy in near]
            acc[j] = acc[j] + jnp.dot(rows, jnp.concatenate(blocks, 0), preferred_element_type=F32)
    shape = (out_ref.shape[0], out_ref.shape[2], DH)
    for j in range(4):
        at = slice((j % 2) * DH, (j % 2 + 1) * DH)
        out_ref[:, c if j < 2 else 1 - c, :, at] = acc[j].astype(BF).reshape(shape)


def project(where, pieces, weights):
    out = jax.ShapeDtypeStruct((8, 2, pieces[0].shape[0] // 8, 2 * DH), BF)
    return kernel_call(project_kernel, [out], where, *pieces, *weights)[0]


def attend_kernel(chunk, last, where_ref, q_ref, kv_ref, *refs):
    length, base = where_ref[0], where_ref[1]
    rows = kv_ref.shape[0]
    per = rows // 16
    if last:
        acc_in, stats_in, outs = refs[0], refs[1], refs[2:]
    else:
        acc_out, stats_out = refs
    row = lax.broadcasted_iota(jnp.int32, (rows, 128), 0)
    shift = per.bit_length() - 1
    position = (row >> (shift + 1)) * 512 + base + ((row >> shift) & 1) * 64 + chunk * per + (row & (per - 1))
    bias = jnp.where(position < length, 0.0, -1e30)
    bias = jnp.concatenate([bias, bias], axis=1)
    keys = kv_ref[:, :DH]
    values = kv_ref[:, DH:].T
    for i in range(8):
        group = where_ref[2 + i // 2] * 2 + i % 2
        q = q_ref[pl.ds(pl.multiple_of(group * 256, 256), 256)]
        s = lax.dot_general(keys, q, (((1,), (1,)), ((), ())), preferred_element_type=F32) + bias
        high = jnp.max(s, axis=0, keepdims=True)
        if last:
            before = stats_in[i, 0:1]
            high = jnp.maximum(high, before)
        p = jnp.exp2((s - high) * EXP_SCALE)
        total = jnp.sum(p, axis=0, keepdims=True)
        acc = jnp.dot(values, p.astype(BF), preferred_element_type=F32)
        if not last:
            acc_out[i] = acc
            stats_out[i] = jnp.concatenate([high, total, jnp.zeros((6, 256), F32)], 0)
            continue
        keep = jnp.exp2((before - high) * EXP_SCALE)
        total = total + stats_in[i, 1:2] * keep
        acc = acc + acc_in[i] * keep
        lse = high * EXP_SCALE + jnp.log2(total)
        first = lse.astype(BF).astype(F32)
        second = (lse - first).astype(BF).astype(F32)
        stats = jnp.concatenate([first, second, lse - first - second, jnp.zeros((13, 256), F32)], 0)
        outs[i // 2][i % 2, :DH] = (acc * (1.0 / total)).astype(BF)
        outs[i // 2][i % 2, DH:] = stats.astype(BF)


def attend(where, q, kv, chunk, before=None):
    last = before is not None
    if last:
        outs = [jax.ShapeDtypeStruct((2, DH + 16, 256), BF)] * 4
    else:
        outs = [jax.ShapeDtypeStruct((8, DH, 256), F32), jax.ShapeDtypeStruct((8, 8, 256), F32)]
    kernel = functools.partial(attend_kernel, chunk, last)
    return kernel_call(kernel, outs, where, q, kv, *(before or ()))


def merge_kernel(where_ref, a_ref, b_ref, c_ref, d_ref, *outs):
    zh = where_ref[0]
    refs = (a_ref, b_ref, c_ref, d_ref)
    contexts = []
    for side in range(2):
        stats = [ref[side, DH:].astype(F32) for ref in refs]
        lse = [s[0:1] + s[1:2] + s[2:3] for s in stats]
        high = functools.reduce(jnp.maximum, lse)
        weight = [jnp.exp2(v - high) for v in lse]
        inverse = 1.0 / sum(weight)
        context = sum(ref[side, :DH].astype(F32) * (w * inverse) for ref, w in zip(refs, weight))
        contexts.append(context.T.astype(BF))
    for d in range(4):
        for m in range(4):

            @pl.when(lax.rem(zh + d, 4) == m)
            def _(d=d, m=m):
                for side in range(2):
                    outs[d][side * 64 : (side + 1) * 64] = contexts[side][m * 64 : (m + 1) * 64]


def merge(where, parts):
    return kernel_call(merge_kernel, [jax.ShapeDtypeStruct((128, DH), BF)] * 4, where, *parts)


def output_kernel(where_ref, *refs):
    c = where_ref[3]
    w_ref, out_mine, out_theirs = refs[4:]
    rows = jnp.concatenate([ref[...] for ref in refs[:4]], 1)
    for i in range(8):
        cols = slice(i * 512, (i + 1) * 512)
        acc = jnp.dot(rows, w_ref[:, cols], preferred_element_type=F32)
        low, high = acc[:64], acc[64:]
        out_mine[:, cols] = jnp.where(c == 0, low, high)
        out_theirs[:, cols] = jnp.where(c == 0, high, low)


def output(where, ctx, w):
    return kernel_call(output_kernel, [jax.ShapeDtypeStruct((64, 4096), F32)] * 2, where, *ctx, w)


def finish_kernel(where_ref, mine, other, residual, gain, hidden, normed):
    x = residual[...].astype(F32) + (mine[...] + other[...])
    scale = lax.rsqrt(jnp.mean(x * x, -1, keepdims=True) + 1e-06)
    hidden[...] = x.astype(BF)
    normed[...] = (x * scale * gain[...]).astype(BF)


def finish(where, *args):
    return kernel_call(finish_kernel, [jax.ShapeDtypeStruct(args[2].shape, BF)] * 2, where, *args)


def shards(memory, kv_weight, mem_lengths, queries, out_weight, residual, norm_gain):
    zh, x, yh, yl, zl, c = (lax.axis_index(a) for a in (Z, X, "yh", "yl", "zl", "c"))
    y = yh * 2 + yl
    where = jnp.stack([zh, x, y, c]).astype(jnp.int32)

    mine = pick(kv_weight[:, :512], kv_weight[:, 512:], c)
    theirs = pick(kv_weight[:, 512:], kv_weight[:, :512], c)
    w_c = swap(theirs, "c")
    w_z = swap(mine, "zl")
    w_zc = lax.ppermute(theirs, ("zl", "c"), [(i, 3 - i) for i in range(4)])
    rows = pair(pair(mine, w_c, c), pair(w_z, w_zc, c), zl)
    k_near = beyond(rows[:, :DH], X)
    v_near = beyond(rows[:, DH:], Y)
    k_near = jnp.stack([rows[:, :DH], *k_near])
    v_near = jnp.stack([rows[:, DH:], *v_near])
    k_far = beyond(k_near, Y)
    v_far = beyond(v_near, X)
    wk = jnp.stack([k_near, *k_far])
    wv = jnp.stack([v_near, *v_far])
    weights = (wk, wv, swap(wk, "c"), swap(wv, "c"))

    step = memory.shape[1] // CHUNKS
    half = 4 * step
    chunks = []
    for j in range(CHUNKS):
        own = memory[:, j * step : (j + 1) * step].reshape(8 * step, 1024)
        prev = lax.ppermute(own, Z, FWD)
        nxt = lax.ppermute(own, Z, BWD)
        opp_a = lax.ppermute(prev[:half], Z, FWD)
        opp_b = lax.ppermute(nxt[half:], Z, BWD)
        chunks.append([own, nxt, opp_a, opp_b, prev])

    ow = lax.dynamic_slice(out_weight, (c * DH, (x * 4 + y) * 256), (DH, 256))
    ow = [ow, *beyond(ow, Z)]
    ow = jnp.concatenate(ow, 0)

    ow = lax.all_gather(ow, XY, axis=1, tiled=True)

    other = pick(queries[:, DH:], queries[:, :DH], c)
    other = swap(other, "c")
    q = pair(pick(queries[:, :DH], queries[:, DH:], c), other, c)
    other = swap(q, "zl")
    q = pair(q, other, zl)
    other = swap(q, "yl")
    q = pair(q, other, yl)

    length = lax.dynamic_index_in_dim(mem_lengths, x * 2 + yh, 0, keepdims=False)
    here = yl * 2 + zl
    here = jnp.stack([length, yl * 256 + zl * 128, here, here ^ 1, here ^ 2, here ^ 3]).astype(jnp.int32)
    state = None
    for j, pieces in enumerate(chunks):
        both = project(where, pieces, weights)
        both = lax.all_to_all(both.reshape(16, step, 512), (X, "yh", "c"), 0, 0, tiled=True)
        state = attend(here, q, both.reshape(16 * step, 512), j, state)

    own, to_zl, to_yl, to_both = state
    parts = (
        own,
        swap(to_zl, "zl"),
        swap(to_yl, "yl"),
        lax.ppermute(to_both, ("yl", "zl"), [(i, 3 - i) for i in range(4)]),
    )
    pieces = merge(where, parts)
    ctx = [pieces[0]] + [lax.ppermute(pieces[4 - d], Z, [(i, (i + 4 - d) % 4) for i in range(4)]) for d in (1, 2, 3)]
    mine, theirs = output(where, ctx, ow)
    return tuple(finish(where, mine, swap(theirs, "c"), residual, norm_gain.reshape(1, -1)))


def solution(mesh):
    fine = Mesh(mesh.devices.reshape(4, 4, 2, 2, 2, 2), (Z, X, "yh", "yl", "zl", "c"))
    seq = (X, "yh", "yl", "zl", "c")
    in_specs = (
        P(None, seq, Z),
        P(seq, Z),
        P(),
        P(seq, Z),
        P(Z, None),
        P(seq + (Z,), None),
        P(),
    )
    out_specs = (P(seq + (Z,), None), P(seq + (Z,), None))
    return jax.shard_map(shards, mesh=fine, in_specs=in_specs, out_specs=out_specs, check_vma=False)
```

```python
import functools
import math

import jax
import jax.numpy as jnp
from jax import lax
from jax.experimental import pallas as pl
from jax.experimental.pallas import tpu as pltpu
from jax.sharding import Mesh, PartitionSpec as P


DH = 256
VMEM_LIMIT = 16 << 20
BF = jnp.bfloat16
F32 = jnp.float32
X = "x"
Y = ("yh", "yl")
XY = ("x", "yh", "yl")
Z = "zh"
EXP_SCALE = math.log2(math.e) / math.sqrt(DH)
FWD = [(i, (i + 1) % 4) for i in range(4)]
BWD = [(i, (i + 3) % 4) for i in range(4)]


def swap(a, axis):
    return lax.ppermute(a, axis, [(0, 1), (1, 0)])


def beyond(a, axis):
    return [lax.ppermute(a, axis, [(i, (i + 4 - d) % 4) for i in range(4)]) for d in (1, 2, 3)]


def pair(a, b, index, axis=0):
    return jnp.where(index == 0, jnp.concatenate([a, b], axis), jnp.concatenate([b, a], axis))


def pick(a, b, index):
    return jnp.where(index == 0, a, b)


def kernel_call(kernel, outs, where, *args):
    spec = pl.BlockSpec(memory_space=pltpu.VMEM)
    args = [pltpu.with_memory_space_constraint(a, pltpu.VMEM) for a in args]
    return pl.pallas_call(
        kernel,
        out_shape=outs,
        in_specs=[pl.BlockSpec(memory_space=pltpu.SMEM)] + [spec] * len(args),
        out_specs=[spec] * len(outs),
        compiler_params=pltpu.CompilerParams(vmem_limit_bytes=VMEM_LIMIT),
    )(where, *args)


def project_kernel(where_ref, *refs):
    pieces, (w_mine, w_theirs, out_ref) = refs[:8], refs[8:]
    zh, x, y, c = where_ref[0], where_ref[1], where_ref[2], where_ref[3]
    acc = [jnp.zeros((512, 2 * DH), F32)] * 2
    near = [lax.rem(i + 4 - y, 4) for i in range(4)]
    for dz in range(4):
        dx = lax.rem(zh + dz + 4 - x, 4)
        rows = jnp.concatenate([pieces[2 * dz][...], pieces[2 * dz + 1][...]], 0)
        for j, w in enumerate((w_mine, w_theirs)):
            block = jnp.concatenate([w[dy, dx] for dy in near], 0)
            acc[j] = acc[j] + jnp.dot(rows, block, preferred_element_type=F32)
    out_ref[:, c] = acc[0].astype(BF).reshape(8, 64, 2 * DH)
    out_ref[:, 1 - c] = acc[1].astype(BF).reshape(8, 64, 2 * DH)


def project(where, pieces, weights):
    out = jax.ShapeDtypeStruct((8, 2, 64, 2 * DH), BF)
    return kernel_call(project_kernel, [out], where, *pieces, *weights)[0]


def attend_kernel(where_ref, q_ref, kv_ref, *outs):
    length, base = where_ref[0], where_ref[1]
    rows = kv_ref.shape[0]
    row = lax.broadcasted_iota(jnp.int32, (rows, 128), 0)
    position = (row >> 7) * 512 + base + (row & 127)
    bias = jnp.where(position < length, 0.0, -1e30)
    bias = jnp.concatenate([bias, bias], axis=1)
    keys = kv_ref[:, :DH]
    values = kv_ref[:, DH:].T
    for i in range(8):
        group = where_ref[2 + i // 2] * 2 + i % 2
        q = q_ref[pl.ds(pl.multiple_of(group * 256, 256), 256)]
        s = lax.dot_general(keys, q, (((1,), (1,)), ((), ())), preferred_element_type=F32) + bias
        high = jnp.max(s, axis=0, keepdims=True)
        p = jnp.exp2((s - high) * EXP_SCALE)
        total = jnp.sum(p, axis=0, keepdims=True)
        acc = jnp.dot(values, p.astype(BF), preferred_element_type=F32)
        lse = high * EXP_SCALE + jnp.log2(total)
        first = lse.astype(BF).astype(F32)
        second = (lse - first).astype(BF).astype(F32)
        stats = jnp.concatenate([first, second, lse - first - second, jnp.zeros((13, 256), F32)], 0)
        outs[i // 2][i % 2, :DH] = (acc * (1.0 / total)).astype(BF)
        outs[i // 2][i % 2, DH:] = stats.astype(BF)


def attend(where, q, kv):
    return kernel_call(attend_kernel, [jax.ShapeDtypeStruct((2, DH + 16, 256), BF)] * 4, where, q, kv)


def merge_kernel(where_ref, a_ref, b_ref, c_ref, d_ref, *outs):
    zh = where_ref[0]
    refs = (a_ref, b_ref, c_ref, d_ref)
    contexts = []
    for side in range(2):
        stats = [ref[side, DH:].astype(F32) for ref in refs]
        lse = [s[0:1] + s[1:2] + s[2:3] for s in stats]
        high = functools.reduce(jnp.maximum, lse)
        weight = [jnp.exp2(v - high) for v in lse]
        inverse = 1.0 / sum(weight)
        context = sum(ref[side, :DH].astype(F32) * (w * inverse) for ref, w in zip(refs, weight))
        contexts.append(context.T.astype(BF))
    for d in range(4):
        for m in range(4):

            @pl.when(lax.rem(zh + d, 4) == m)
            def _(d=d, m=m):
                for side in range(2):
                    outs[d][side * 64 : (side + 1) * 64] = contexts[side][m * 64 : (m + 1) * 64]


def merge(where, parts):
    return kernel_call(merge_kernel, [jax.ShapeDtypeStruct((128, DH), BF)] * 4, where, *parts)


def output_kernel(where_ref, *refs):
    c = where_ref[3]
    w_ref, out_mine, out_theirs = refs[4:]
    rows = jnp.concatenate([ref[...] for ref in refs[:4]], 1)
    for i in range(8):
        cols = slice(i * 512, (i + 1) * 512)
        acc = jnp.dot(rows, w_ref[:, cols], preferred_element_type=F32)
        low, high = acc[:64], acc[64:]
        out_mine[:, cols] = jnp.where(c == 0, low, high)
        out_theirs[:, cols] = jnp.where(c == 0, high, low)


def output(where, ctx, w):
    return kernel_call(output_kernel, [jax.ShapeDtypeStruct((64, 4096), F32)] * 2, where, *ctx, w)


def finish_kernel(where_ref, mine, other, residual, gain, hidden, normed):
    x = residual[...].astype(F32) + (mine[...] + other[...])
    scale = lax.rsqrt(jnp.mean(x * x, -1, keepdims=True) + 1e-06)
    hidden[...] = x.astype(BF)
    normed[...] = (x * scale * gain[...]).astype(BF)


def finish(where, *args):
    return kernel_call(finish_kernel, [jax.ShapeDtypeStruct(args[2].shape, BF)] * 2, where, *args)


def shards(memory, kv_weight, mem_lengths, queries, out_weight, residual, norm_gain):
    zh, x, yh, yl, zl, c = (lax.axis_index(a) for a in (Z, X, "yh", "yl", "zl", "c"))
    y = yh * 2 + yl
    where = jnp.stack([zh, x, y, c]).astype(jnp.int32)

    mine = pick(kv_weight[:, :512], kv_weight[:, 512:], c)
    theirs = pick(kv_weight[:, 512:], kv_weight[:, :512], c)
    w_c = swap(theirs, "c")
    w_z = swap(mine, "zl")
    w_zc = lax.ppermute(theirs, ("zl", "c"), [(i, 3 - i) for i in range(4)])
    rows = pair(pair(mine, w_c, c), pair(w_z, w_zc, c), zl)
    w_near = beyond(rows, X)
    w_near = jnp.stack([rows, *w_near])
    w_prev = lax.ppermute(w_near, Y, FWD)
    w_next = lax.ppermute(w_near, Y, BWD)
    w_far_a = lax.ppermute(w_prev[:2], Y, FWD)
    w_far_b = lax.ppermute(w_next[2:], Y, BWD)
    w_mine = jnp.concatenate([w_near, w_next, w_far_a, w_far_b, w_prev], 0).reshape((4,) + w_near.shape)
    w_theirs = swap(w_mine, "c")

    mem_a, mem_b = memory[:4].reshape(256, 1024), memory[4:].reshape(256, 1024)
    prev_a = lax.ppermute(mem_a, Z, FWD)
    next_a = lax.ppermute(mem_a, Z, BWD)
    next_b = lax.ppermute(mem_b, Z, BWD)
    prev_b = lax.ppermute(mem_b, Z, FWD)
    far_a = lax.ppermute(prev_a, Z, FWD)
    far_b = lax.ppermute(next_b, Z, BWD)
    pieces = (mem_a, mem_b, next_a, next_b, far_a, far_b, prev_a, prev_b)

    ow = lax.dynamic_slice(out_weight, (c * DH, (x * 4 + y) * 256), (DH, 256))
    ow = [ow, *beyond(ow, Z)]
    ow = jnp.concatenate(ow, 0)

    ow = lax.all_gather(ow, XY, axis=1, tiled=True)

    other = pick(queries[:, DH:], queries[:, :DH], c)
    other = swap(other, "c")
    q = pair(pick(queries[:, :DH], queries[:, DH:], c), other, c)
    other = swap(q, "zl")
    q = pair(q, other, zl)
    other = swap(q, "yl")
    q = pair(q, other, yl)

    length = lax.dynamic_index_in_dim(mem_lengths, x * 2 + yh, 0, keepdims=False)
    here = yl * 2 + zl
    here = jnp.stack([length, yl * 256 + zl * 128, here, here ^ 1, here ^ 2, here ^ 3]).astype(jnp.int32)
    both = project(where, pieces, (w_mine, w_theirs))
    both = lax.all_to_all(both.reshape(16, 64, 512), (X, "yh", "c"), 0, 0, tiled=True)
    own, to_zl, to_yl, to_both = attend(here, q, both.reshape(1024, 512))

    parts = (
        own,
        swap(to_zl, "zl"),
        swap(to_yl, "yl"),
        lax.ppermute(to_both, ("yl", "zl"), [(i, 3 - i) for i in range(4)]),
    )
    pieces = merge(where, parts)
    ctx = [pieces[0]] + [lax.ppermute(pieces[4 - d], Z, [(i, (i + 4 - d) % 4) for i in range(4)]) for d in (1, 2, 3)]
    mine, theirs = output(where, ctx, ow)
    return tuple(finish(where, mine, swap(theirs, "c"), residual, norm_gain.reshape(1, -1)))


def solution(mesh):
    fine = Mesh(mesh.devices.reshape(4, 4, 2, 2, 2, 2), (Z, X, "yh", "yl", "zl", "c"))
    seq = (X, "yh", "yl", "zl", "c")
    in_specs = (
        P(None, seq, Z),
        P(seq, Z),
        P(),
        P(seq, Z),
        P(Z, None),
        P(seq + (Z,), None),
        P(),
    )
    out_specs = (P(seq + (Z,), None), P(seq + (Z,), None))
    return jax.shard_map(shards, mesh=fine, in_specs=in_specs, out_specs=out_specs, check_vma=False)
```

```python
import functools
import math

import jax
import jax.numpy as jnp
from jax import lax
from jax.experimental import pallas as pl
from jax.experimental.pallas import tpu as pltpu
from jax.sharding import Mesh, PartitionSpec as P


DH = 256
VMEM_LIMIT = 16 << 20
BF = jnp.bfloat16
F32 = jnp.float32
X = "x"
Y = ("yh", "yl")
Z = "zh"
EXP_SCALE = math.log2(math.e) / math.sqrt(DH)
FWD = [(i, (i + 1) % 4) for i in range(4)]
BWD = [(i, (i + 3) % 4) for i in range(4)]


def swap(a, axis):
    return lax.ppermute(a, axis, [(0, 1), (1, 0)])


def beyond(a, axis):
    return [lax.ppermute(a, axis, [(i, (i + 4 - d) % 4) for i in range(4)]) for d in (1, 2, 3)]


def pair(a, b, index, axis=0):
    return jnp.where(index == 0, jnp.concatenate([a, b], axis), jnp.concatenate([b, a], axis))


def pick(a, b, index):
    return jnp.where(index == 0, a, b)


def kernel_call(kernel, outs, where, *args):
    spec = pl.BlockSpec(memory_space=pltpu.VMEM)
    args = [pltpu.with_memory_space_constraint(a, pltpu.VMEM) for a in args]
    return pl.pallas_call(
        kernel,
        out_shape=outs,
        in_specs=[pl.BlockSpec(memory_space=pltpu.SMEM)] + [spec] * len(args),
        out_specs=[spec] * len(outs),
        compiler_params=pltpu.CompilerParams(vmem_limit_bytes=VMEM_LIMIT),
    )(where, *args)


def project_kernel(where_ref, *refs):
    pieces, (w_mine, w_theirs, out_ref) = refs[:8], refs[8:]
    zh, x, y, c = where_ref[0], where_ref[1], where_ref[2], where_ref[3]
    acc = [jnp.zeros((512, 2 * DH), F32)] * 2
    near = [lax.rem(i + 4 - y, 4) for i in range(4)]
    for dz in range(4):
        dx = lax.rem(zh + dz + 4 - x, 4)
        rows = jnp.concatenate([pieces[2 * dz][...], pieces[2 * dz + 1][...]], 0)
        for j, w in enumerate((w_mine, w_theirs)):
            block = jnp.concatenate([w[dy, dx] for dy in near], 0)
            acc[j] = acc[j] + jnp.dot(rows, block, preferred_element_type=F32)
    out_ref[:, c] = acc[0].astype(BF).reshape(8, 64, 2 * DH)
    out_ref[:, 1 - c] = acc[1].astype(BF).reshape(8, 64, 2 * DH)


def project(where, pieces, weights):
    out = jax.ShapeDtypeStruct((8, 2, 64, 2 * DH), BF)
    return kernel_call(project_kernel, [out], where, *pieces, *weights)[0]


def attend_kernel(where_ref, q_ref, kv_ref, *outs):
    length, base = where_ref[0], where_ref[1]
    rows = kv_ref.shape[0]
    row = lax.broadcasted_iota(jnp.int32, (rows, 128), 0)
    position = (row >> 7) * 512 + base + (row & 127)
    bias = jnp.where(position < length, 0.0, -1e30)
    bias = jnp.concatenate([bias, bias], axis=1)
    keys = kv_ref[:, :DH]
    values = kv_ref[:, DH:].T
    for i in range(8):
        group = where_ref[2 + i // 2] * 2 + i % 2
        q = q_ref[pl.ds(pl.multiple_of(group * 256, 256), 256)]
        s = lax.dot_general(keys, q, (((1,), (1,)), ((), ())), preferred_element_type=F32) + bias
        high = jnp.max(s, axis=0, keepdims=True)
        p = jnp.exp2((s - high) * EXP_SCALE)
        total = jnp.sum(p, axis=0, keepdims=True)
        acc = jnp.dot(values, p.astype(BF), preferred_element_type=F32)
        lse = high * EXP_SCALE + jnp.log2(total)
        first = lse.astype(BF).astype(F32)
        second = (lse - first).astype(BF).astype(F32)
        stats = jnp.concatenate([first, second, lse - first - second, jnp.zeros((13, 256), F32)], 0)
        outs[i // 2][i % 2, :DH] = (acc * (1.0 / total)).astype(BF)
        outs[i // 2][i % 2, DH:] = stats.astype(BF)


def attend(where, q, kv):
    return kernel_call(attend_kernel, [jax.ShapeDtypeStruct((2, DH + 16, 256), BF)] * 4, where, q, kv)


def merge_kernel(where_ref, a_ref, b_ref, c_ref, d_ref, *outs):
    refs = (a_ref, b_ref, c_ref, d_ref)
    contexts = []
    for side in range(2):
        stats = [ref[side, DH:].astype(F32) for ref in refs]
        lse = [s[0:1] + s[1:2] + s[2:3] for s in stats]
        high = functools.reduce(jnp.maximum, lse)
        weight = [jnp.exp2(v - high) for v in lse]
        inverse = 1.0 / sum(weight)
        context = sum(ref[side, :DH].astype(F32) * (w * inverse) for ref, w in zip(refs, weight))
        contexts.append(context.T.astype(BF))
    c = where_ref[3]
    outs[0][...] = jnp.where(c == 0, contexts[0], contexts[1])
    outs[1][...] = jnp.where(c == 0, contexts[1], contexts[0])


def merge(where, parts):
    return kernel_call(merge_kernel, [jax.ShapeDtypeStruct((256, DH), BF)] * 2, where, *parts)


def output_kernel(where_ref, mine, theirs, w_ref, own, fwd_a, fwd_b, bwd_a, bwd_b, far_a, far_b):
    zh, c = where_ref[0], where_ref[3]

    def by_distance(ref):
        return jnp.concatenate([ref[pl.ds(pl.multiple_of(lax.rem(zh + d, 4) * 64, 64), 64)] for d in range(4)], 0)

    rows = (by_distance(mine), by_distance(theirs))
    heads = [pl.ds(pl.multiple_of(h * DH, DH), DH) for h in (c, 1 - c)]
    for i in range(8):
        cols = slice(i * 512, (i + 1) * 512)
        acc = sum(jnp.dot(r, w_ref[h, cols], preferred_element_type=F32) for r, h in zip(rows, heads))
        own[:, cols] = acc[:64]
        for at, out in ((64, fwd_a), (96, fwd_b), (128, far_a), (160, far_b), (192, bwd_a), (224, bwd_b)):
            out[:, cols] = acc[at : at + 32].astype(out.dtype)


def output(where, mine, theirs, w):
    outs = [jax.ShapeDtypeStruct((64, 4096), F32)]
    outs += [jax.ShapeDtypeStruct((32, 4096), t) for t in (F32, BF, BF, F32, BF, BF)]
    return kernel_call(output_kernel, outs, where, mine, theirs, w)


def finish_kernel(where_ref, own, prev_a, prev_b, next_a, next_b, residual, gain, hidden, normed):
    for at, left, right in ((0, prev_a, next_a), (32, prev_b, next_b)):
        rows = slice(at, at + 32)
        x = residual[rows].astype(F32) + (own[rows] + (left[...].astype(F32) + right[...].astype(F32)))
        scale = lax.rsqrt(jnp.mean(x * x, -1, keepdims=True) + 1e-06)
        hidden[rows] = x.astype(BF)
        normed[rows] = (x * scale * gain[...]).astype(BF)


def finish(where, *args):
    return kernel_call(finish_kernel, [jax.ShapeDtypeStruct((64, 4096), BF)] * 2, where, *args)


def shards(memory, kv_weight, mem_lengths, queries, out_weight, residual, norm_gain):
    zh, x, yh, yl, zl, c = (lax.axis_index(a) for a in (Z, X, "yh", "yl", "zl", "c"))
    y = yh * 2 + yl
    where = jnp.stack([zh, x, y, c]).astype(jnp.int32)

    mine = pick(kv_weight[:, :512], kv_weight[:, 512:], c)
    theirs = pick(kv_weight[:, 512:], kv_weight[:, :512], c)
    w_c = swap(theirs, "c")
    w_z = swap(mine, "zl")
    w_zc = lax.ppermute(theirs, ("zl", "c"), [(i, 3 - i) for i in range(4)])
    rows = pair(pair(mine, w_c, c), pair(w_z, w_zc, c), zl)
    w_near = beyond(rows, X)
    w_near = jnp.stack([rows, *w_near])
    w_prev = lax.ppermute(w_near, Y, FWD)
    w_next = lax.ppermute(w_near, Y, BWD)
    w_far_a = lax.ppermute(w_prev[:2], Y, FWD)
    w_far_b = lax.ppermute(w_next[2:], Y, BWD)
    w_mine = jnp.concatenate([w_near, w_next, w_far_a, w_far_b, w_prev], 0).reshape((4,) + w_near.shape)
    w_theirs = swap(w_mine, "c")

    mem_a, mem_b = memory[:4].reshape(256, 1024), memory[4:].reshape(256, 1024)
    prev_a = lax.ppermute(mem_a, Z, FWD)
    next_a = lax.ppermute(mem_a, Z, BWD)
    next_b = lax.ppermute(mem_b, Z, BWD)
    prev_b = lax.ppermute(mem_b, Z, FWD)
    far_a = lax.ppermute(prev_a, Z, FWD)
    far_b = lax.ppermute(next_b, Z, BWD)
    pieces = (mem_a, mem_b, next_a, next_b, far_a, far_b, prev_a, prev_b)

    other = pick(queries[:, DH:], queries[:, :DH], c)
    other = swap(other, "c")
    q = pair(pick(queries[:, :DH], queries[:, DH:], c), other, c)
    other = swap(q, "zl")
    q = pair(q, other, zl)
    other = swap(q, "yl")
    q = pair(q, other, yl)

    length = lax.dynamic_index_in_dim(mem_lengths, x * 2 + yh, 0, keepdims=False)
    here = yl * 2 + zl
    here = jnp.stack([length, yl * 256 + zl * 128, here, here ^ 1, here ^ 2, here ^ 3]).astype(jnp.int32)
    both = project(where, pieces, (w_mine, w_theirs))
    both = lax.all_to_all(both.reshape(16, 64, 512), (X, "yh", "c"), 0, 0, tiled=True)
    own, to_zl, to_yl, to_both = attend(here, q, both.reshape(1024, 512))

    parts = (
        own,
        swap(to_zl, "zl"),
        swap(to_yl, "yl"),
        lax.ppermute(to_both, ("yl", "zl"), [(i, 3 - i) for i in range(4)]),
    )
    mine, theirs = merge(where, parts)
    own, fwd_a, fwd_b, bwd_a, bwd_b, far_a, far_b = output(where, mine, swap(theirs, "c"), out_weight)

    far_a = lax.ppermute(far_a, Z, FWD)
    far_b = lax.ppermute(far_b, Z, BWD)
    prev_b = lax.ppermute(fwd_b, Z, FWD)
    next_a = lax.ppermute(bwd_a, Z, BWD)
    fwd_a = (fwd_a + far_a.astype(F32)).astype(BF)
    bwd_b = (bwd_b + far_b.astype(F32)).astype(BF)
    prev_a = lax.ppermute(fwd_a, Z, FWD)
    next_b = lax.ppermute(bwd_b, Z, BWD)
    return tuple(finish(where, own, prev_a, prev_b, next_a, next_b, residual, norm_gain.reshape(1, -1)))


def solution(mesh):
    fine = Mesh(mesh.devices.reshape(4, 4, 2, 2, 2, 2), (Z, X, "yh", "yl", "zl", "c"))
    seq = (X, "yh", "yl", "zl", "c")
    in_specs = (
        P(None, seq, Z),
        P(seq, Z),
        P(),
        P(seq, Z),
        P(Z, None),
        P(seq + (Z,), None),
        P(),
    )
    out_specs = (P(seq + (Z,), None), P(seq + (Z,), None))
    return jax.shard_map(shards, mesh=fine, in_specs=in_specs, out_specs=out_specs, check_vma=False)
```

```python
import functools
import math

import jax
import jax.numpy as jnp
from jax import lax
from jax.experimental import pallas as pl
from jax.experimental.pallas import tpu as pltpu
from jax.sharding import Mesh, PartitionSpec as P


DH = 256
VMEM_LIMIT = 16 << 20
BF = jnp.bfloat16
F32 = jnp.float32
X = "x"
Y = ("yh", "yl")
Z = "zh"
EXP_SCALE = math.log2(math.e) / math.sqrt(DH)
FWD = [(i, (i + 1) % 4) for i in range(4)]
BWD = [(i, (i + 3) % 4) for i in range(4)]


def swap(a, axis):
    return lax.ppermute(a, axis, [(0, 1), (1, 0)])


def beyond(a, axis):
    return [lax.ppermute(a, axis, [(i, (i + 4 - d) % 4) for i in range(4)]) for d in (1, 2, 3)]


def pair(a, b, index, axis=0):
    return jnp.where(index == 0, jnp.concatenate([a, b], axis), jnp.concatenate([b, a], axis))


def pick(a, b, index):
    return jnp.where(index == 0, a, b)


def kernel_call(kernel, outs, where, *args, far=(), scratch=()):
    spec = pl.BlockSpec(memory_space=pltpu.VMEM)
    args = [pltpu.with_memory_space_constraint(a, pltpu.VMEM) for a in args]
    return pl.pallas_call(
        kernel,
        out_shape=outs,
        in_specs=[pl.BlockSpec(memory_space=pltpu.SMEM)]
        + [spec] * len(args)
        + [pl.BlockSpec(memory_space=pl.ANY)] * len(far),
        out_specs=[spec] * len(outs),
        scratch_shapes=scratch,
        compiler_params=pltpu.CompilerParams(vmem_limit_bytes=VMEM_LIMIT),
    )(where, *args, *far)


def project_kernel(where_ref, *refs):
    pieces, (w_mine, w_theirs, out_ref) = refs[:8], refs[8:]
    zh, x, y, c = where_ref[0], where_ref[1], where_ref[2], where_ref[3]
    acc = [jnp.zeros((512, 2 * DH), F32)] * 2
    near = [lax.rem(i + 4 - y, 4) for i in range(4)]
    for dz in range(4):
        dx = lax.rem(zh + dz + 4 - x, 4)
        rows = jnp.concatenate([pieces[2 * dz][...], pieces[2 * dz + 1][...]], 0)
        for j, w in enumerate((w_mine, w_theirs)):
            block = jnp.concatenate([w[dy, dx] for dy in near], 0)
            acc[j] = acc[j] + jnp.dot(rows, block, preferred_element_type=F32)
    out_ref[:, c] = acc[0].astype(BF).reshape(8, 64, 2 * DH)
    out_ref[:, 1 - c] = acc[1].astype(BF).reshape(8, 64, 2 * DH)


def project(where, pieces, weights):
    out = jax.ShapeDtypeStruct((8, 2, 64, 2 * DH), BF)
    return kernel_call(project_kernel, [out], where, *pieces, *weights)[0]


def attend_kernel(where_ref, q_ref, kv_ref, *outs):
    length, base = where_ref[0], where_ref[1]
    rows = kv_ref.shape[0]
    row = lax.broadcasted_iota(jnp.int32, (rows, 128), 0)
    position = (row >> 7) * 512 + base + (row & 127)
    bias = jnp.where(position < length, 0.0, -1e30)
    bias = jnp.concatenate([bias, bias], axis=1)
    keys = kv_ref[:, :DH]
    values = kv_ref[:, DH:].T
    for i in range(8):
        group = where_ref[2 + i // 2] * 2 + i % 2
        q = q_ref[pl.ds(pl.multiple_of(group * 256, 256), 256)]
        s = lax.dot_general(keys, q, (((1,), (1,)), ((), ())), preferred_element_type=F32) + bias
        high = jnp.max(s, axis=0, keepdims=True)
        p = jnp.exp2((s - high) * EXP_SCALE)
        total = jnp.sum(p, axis=0, keepdims=True)
        acc = jnp.dot(values, p.astype(BF), preferred_element_type=F32)
        lse = high * EXP_SCALE + jnp.log2(total)
        first = lse.astype(BF).astype(F32)
        second = (lse - first).astype(BF).astype(F32)
        stats = jnp.concatenate([first, second, lse - first - second, jnp.zeros((13, 256), F32)], 0)
        outs[i // 2][i % 2, :DH] = (acc * (1.0 / total)).astype(BF)
        outs[i // 2][i % 2, DH:] = stats.astype(BF)


def attend(where, q, kv):
    return kernel_call(attend_kernel, [jax.ShapeDtypeStruct((2, DH + 16, 256), BF)] * 4, where, q, kv)


def merge_kernel(where_ref, a_ref, b_ref, c_ref, d_ref, *outs):
    refs = (a_ref, b_ref, c_ref, d_ref)
    contexts = []
    for side in range(2):
        stats = [ref[side, DH:].astype(F32) for ref in refs]
        lse = [s[0:1] + s[1:2] + s[2:3] for s in stats]
        high = functools.reduce(jnp.maximum, lse)
        weight = [jnp.exp2(v - high) for v in lse]
        inverse = 1.0 / sum(weight)
        context = sum(ref[side, :DH].astype(F32) * (w * inverse) for ref, w in zip(refs, weight))
        contexts.append(context.T.astype(BF))
    c = where_ref[3]
    outs[0][...] = jnp.where(c == 0, contexts[0], contexts[1])
    outs[1][...] = jnp.where(c == 0, contexts[1], contexts[0])


def merge(where, parts):
    return kernel_call(merge_kernel, [jax.ShapeDtypeStruct((256, DH), BF)] * 2, where, *parts)


def output_kernel(where_ref, mine, theirs, w_ref, own, fwd_a, fwd_b, bwd_a, bwd_b, far_a, far_b, buf, sem):
    zh, c = where_ref[0], where_ref[3]
    copies = [pltpu.make_async_copy(w_ref.at[:, pl.ds(i * 512, 512)], buf.at[i], sem.at[i]) for i in range(8)]
    for copy in copies:
        copy.start()

    def by_distance(ref):
        return jnp.concatenate([ref[pl.ds(pl.multiple_of(lax.rem(zh + d, 4) * 64, 64), 64)] for d in range(4)], 0)

    rows = (by_distance(mine), by_distance(theirs))
    heads = [pl.ds(pl.multiple_of(h * DH, DH), DH) for h in (c, 1 - c)]
    for i in range(8):
        cols = slice(i * 512, (i + 1) * 512)
        copies[i].wait()
        acc = sum(jnp.dot(r, buf[i, h], preferred_element_type=F32) for r, h in zip(rows, heads))
        own[:, cols] = acc[:64]
        for at, out in ((64, fwd_a), (96, fwd_b), (128, far_a), (160, far_b), (192, bwd_a), (224, bwd_b)):
            out[:, cols] = acc[at : at + 32].astype(out.dtype)


def output(where, mine, theirs, w):
    outs = [jax.ShapeDtypeStruct((64, 4096), F32)]
    outs += [jax.ShapeDtypeStruct((32, 4096), t) for t in (F32, BF, BF, F32, BF, BF)]
    scratch = [pltpu.VMEM((8, 512, 512), BF), pltpu.SemaphoreType.DMA((8,))]
    return kernel_call(output_kernel, outs, where, mine, theirs, far=(w,), scratch=scratch)


def finish_kernel(where_ref, own, prev_a, prev_b, next_a, next_b, residual, gain, hidden, normed):
    for at, left, right in ((0, prev_a, next_a), (32, prev_b, next_b)):
        rows = slice(at, at + 32)
        x = residual[rows].astype(F32) + (own[rows] + (left[...].astype(F32) + right[...].astype(F32)))
        scale = lax.rsqrt(jnp.mean(x * x, -1, keepdims=True) + 1e-06)
        hidden[rows] = x.astype(BF)
        normed[rows] = (x * scale * gain[...]).astype(BF)


def finish(where, *args):
    return kernel_call(finish_kernel, [jax.ShapeDtypeStruct((64, 4096), BF)] * 2, where, *args)


def shards(memory, kv_weight, mem_lengths, queries, out_weight, residual, norm_gain):
    zh, x, yh, yl, zl, c = (lax.axis_index(a) for a in (Z, X, "yh", "yl", "zl", "c"))
    y = yh * 2 + yl
    where = jnp.stack([zh, x, y, c]).astype(jnp.int32)

    mine = pick(kv_weight[:, :512], kv_weight[:, 512:], c)
    theirs = pick(kv_weight[:, 512:], kv_weight[:, :512], c)
    w_c = swap(theirs, "c")
    w_z = swap(mine, "zl")
    w_zc = lax.ppermute(theirs, ("zl", "c"), [(i, 3 - i) for i in range(4)])
    rows = pair(pair(mine, w_c, c), pair(w_z, w_zc, c), zl)
    w_near = beyond(rows, X)
    w_near = jnp.stack([rows, *w_near])
    w_prev = lax.ppermute(w_near, Y, FWD)
    w_next = lax.ppermute(w_near, Y, BWD)
    w_far_a = lax.ppermute(w_prev[:2], Y, FWD)
    w_far_b = lax.ppermute(w_next[2:], Y, BWD)
    w_mine = jnp.concatenate([w_near, w_next, w_far_a, w_far_b, w_prev], 0).reshape((4,) + w_near.shape)
    w_theirs = swap(w_mine, "c")

    mem_a, mem_b = memory[:4].reshape(256, 1024), memory[4:].reshape(256, 1024)
    prev_a = lax.ppermute(mem_a, Z, FWD)
    next_a = lax.ppermute(mem_a, Z, BWD)
    next_b = lax.ppermute(mem_b, Z, BWD)
    prev_b = lax.ppermute(mem_b, Z, FWD)
    far_a = lax.ppermute(prev_a, Z, FWD)
    far_b = lax.ppermute(next_b, Z, BWD)
    pieces = (mem_a, mem_b, next_a, next_b, far_a, far_b, prev_a, prev_b)

    other = pick(queries[:, DH:], queries[:, :DH], c)
    other = swap(other, "c")
    q = pair(pick(queries[:, :DH], queries[:, DH:], c), other, c)
    other = swap(q, "zl")
    q = pair(q, other, zl)
    other = swap(q, "yl")
    q = pair(q, other, yl)

    length = lax.dynamic_index_in_dim(mem_lengths, x * 2 + yh, 0, keepdims=False)
    here = yl * 2 + zl
    here = jnp.stack([length, yl * 256 + zl * 128, here, here ^ 1, here ^ 2, here ^ 3]).astype(jnp.int32)
    both = project(where, pieces, (w_mine, w_theirs))
    both = lax.all_to_all(both.reshape(16, 64, 512), (X, "yh", "c"), 0, 0, tiled=True)
    own, to_zl, to_yl, to_both = attend(here, q, both.reshape(1024, 512))

    parts = (
        own,
        swap(to_zl, "zl"),
        swap(to_yl, "yl"),
        lax.ppermute(to_both, ("yl", "zl"), [(i, 3 - i) for i in range(4)]),
    )
    mine, theirs = merge(where, parts)
    own, fwd_a, fwd_b, bwd_a, bwd_b, far_a, far_b = output(where, mine, swap(theirs, "c"), out_weight)

    far_a = lax.ppermute(far_a, Z, FWD)
    far_b = lax.ppermute(far_b, Z, BWD)
    prev_b = lax.ppermute(fwd_b, Z, FWD)
    next_a = lax.ppermute(bwd_a, Z, BWD)
    fwd_a = (fwd_a + far_a.astype(F32)).astype(BF)
    bwd_b = (bwd_b + far_b.astype(F32)).astype(BF)
    prev_a = lax.ppermute(fwd_a, Z, FWD)
    next_b = lax.ppermute(bwd_b, Z, BWD)
    return tuple(finish(where, own, prev_a, prev_b, next_a, next_b, residual, norm_gain.reshape(1, -1)))


def solution(mesh):
    fine = Mesh(mesh.devices.reshape(4, 4, 2, 2, 2, 2), (Z, X, "yh", "yl", "zl", "c"))
    seq = (X, "yh", "yl", "zl", "c")
    in_specs = (
        P(None, seq, Z),
        P(seq, Z),
        P(),
        P(seq, Z),
        P(Z, None),
        P(seq + (Z,), None),
        P(),
    )
    out_specs = (P(seq + (Z,), None), P(seq + (Z,), None))
    return jax.shard_map(shards, mesh=fine, in_specs=in_specs, out_specs=out_specs, check_vma=False)
```

```python
import functools
import math

import jax
import jax.numpy as jnp
from jax import lax
from jax.experimental import pallas as pl
from jax.experimental.pallas import tpu as pltpu
from jax.sharding import Mesh, PartitionSpec as P


DH = 256
VMEM_LIMIT = 16 << 20
BF = jnp.bfloat16
F32 = jnp.float32
X = "x"
Y = ("yh", "yl")
Z = "zh"
EXP_SCALE = math.log2(math.e) / math.sqrt(DH)
FWD = [(i, (i + 1) % 4) for i in range(4)]
BWD = [(i, (i + 3) % 4) for i in range(4)]


def swap(a, axis):
    return lax.ppermute(a, axis, [(0, 1), (1, 0)])


def beyond(a, axis):
    return [lax.ppermute(a, axis, [(i, (i + 4 - d) % 4) for i in range(4)]) for d in (1, 2, 3)]


def pair(a, b, index, axis=0):
    return jnp.where(index == 0, jnp.concatenate([a, b], axis), jnp.concatenate([b, a], axis))


def pick(a, b, index):
    return jnp.where(index == 0, a, b)


def kernel_call(kernel, outs, where, *args):
    spec = pl.BlockSpec(memory_space=pltpu.VMEM)
    args = [pltpu.with_memory_space_constraint(a, pltpu.VMEM) for a in args]
    return pl.pallas_call(
        kernel,
        out_shape=outs,
        in_specs=[pl.BlockSpec(memory_space=pltpu.SMEM)] + [spec] * len(args),
        out_specs=[spec] * len(outs),
        compiler_params=pltpu.CompilerParams(vmem_limit_bytes=VMEM_LIMIT),
    )(where, *args)


def project_kernel(where_ref, own, nxt, opp_a, opp_b, prev, w_mine, w_theirs, out_ref):
    zh, x, y, c = where_ref[0], where_ref[1], where_ref[2], where_ref[3]
    acc = [jnp.zeros((own.shape[0], 2 * DH), F32)] * 2
    near = [lax.rem(i + 4 - y, 4) for i in range(4)]
    for dz in range(4):
        dx = lax.rem(zh + dz + 4 - x, 4)
        if dz == 2:
            rows = jnp.concatenate([opp_a[...], opp_b[...]], 0)
        else:
            rows = (own, nxt, None, prev)[dz][...]
        for j, w in enumerate((w_mine, w_theirs)):
            block = jnp.concatenate([w[dy, dx] for dy in near], 0)
            acc[j] = acc[j] + jnp.dot(rows, block, preferred_element_type=F32)
    shape = (out_ref.shape[0],) + out_ref.shape[2:]
    out_ref[:, c] = acc[0].astype(BF).reshape(shape)
    out_ref[:, 1 - c] = acc[1].astype(BF).reshape(shape)


def project(where, pieces, weights):
    out = jax.ShapeDtypeStruct((8, 2, pieces[0].shape[0] // 8, 2 * DH), BF)
    return kernel_call(project_kernel, [out], where, *pieces, *weights)[0]


def attend_kernel(chunk, last, where_ref, q_ref, kv_ref, *refs):
    length, base = where_ref[0], where_ref[1]
    rows = kv_ref.shape[0]
    per = rows // 16
    if last:
        acc_in, stats_in, outs = refs[0], refs[1], refs[2:]
    else:
        acc_out, stats_out = refs
    row = lax.broadcasted_iota(jnp.int32, (rows, 128), 0)
    shift = per.bit_length() - 1
    position = (row >> (shift + 1)) * 512 + base + ((row >> shift) & 1) * 64 + chunk * per + (row & (per - 1))
    bias = jnp.where(position < length, 0.0, -1e30)
    bias = jnp.concatenate([bias, bias], axis=1)
    keys = kv_ref[:, :DH]
    values = kv_ref[:, DH:].T
    for i in range(8):
        group = where_ref[2 + i // 2] * 2 + i % 2
        q = q_ref[pl.ds(pl.multiple_of(group * 256, 256), 256)]
        s = lax.dot_general(keys, q, (((1,), (1,)), ((), ())), preferred_element_type=F32) + bias
        high = jnp.max(s, axis=0, keepdims=True)
        if last:
            before = stats_in[i, 0:1]
            high = jnp.maximum(high, before)
        p = jnp.exp2((s - high) * EXP_SCALE)
        total = jnp.sum(p, axis=0, keepdims=True)
        acc = jnp.dot(values, p.astype(BF), preferred_element_type=F32)
        if not last:
            acc_out[i] = acc
            stats_out[i] = jnp.concatenate([high, total, jnp.zeros((6, 256), F32)], 0)
            continue
        keep = jnp.exp2((before - high) * EXP_SCALE)
        total = total + stats_in[i, 1:2] * keep
        acc = acc + acc_in[i] * keep
        lse = high * EXP_SCALE + jnp.log2(total)
        first = lse.astype(BF).astype(F32)
        second = (lse - first).astype(BF).astype(F32)
        stats = jnp.concatenate([first, second, lse - first - second, jnp.zeros((13, 256), F32)], 0)
        outs[i // 2][i % 2, :DH] = (acc * (1.0 / total)).astype(BF)
        outs[i // 2][i % 2, DH:] = stats.astype(BF)


def attend(where, q, kv, chunk, before=None):
    last = before is not None
    if last:
        outs = [jax.ShapeDtypeStruct((2, DH + 16, 256), BF)] * 4
    else:
        outs = [jax.ShapeDtypeStruct((8, DH, 256), F32), jax.ShapeDtypeStruct((8, 8, 256), F32)]
    kernel = functools.partial(attend_kernel, chunk, last)
    return kernel_call(kernel, outs, where, q, kv, *(before or ()))


def merge_kernel(where_ref, a_ref, b_ref, c_ref, d_ref, *outs):
    refs = (a_ref, b_ref, c_ref, d_ref)
    contexts = []
    for side in range(2):
        stats = [ref[side, DH:].astype(F32) for ref in refs]
        lse = [s[0:1] + s[1:2] + s[2:3] for s in stats]
        high = functools.reduce(jnp.maximum, lse)
        weight = [jnp.exp2(v - high) for v in lse]
        inverse = 1.0 / sum(weight)
        context = sum(ref[side, :DH].astype(F32) * (w * inverse) for ref, w in zip(refs, weight))
        contexts.append(context.T.astype(BF))
    c = where_ref[3]
    outs[0][...] = jnp.where(c == 0, contexts[0], contexts[1])
    outs[1][...] = jnp.where(c == 0, contexts[1], contexts[0])


def merge(where, parts):
    return kernel_call(merge_kernel, [jax.ShapeDtypeStruct((256, DH), BF)] * 2, where, *parts)


def output_kernel(where_ref, mine, theirs, w_ref, own, fwd_a, fwd_b, bwd_a, bwd_b, far_a, far_b):
    zh, c = where_ref[0], where_ref[3]

    def by_distance(ref):
        return jnp.concatenate([ref[pl.ds(pl.multiple_of(lax.rem(zh + d, 4) * 64, 64), 64)] for d in range(4)], 0)

    rows = (by_distance(mine), by_distance(theirs))
    heads = [pl.ds(pl.multiple_of(h * DH, DH), DH) for h in (c, 1 - c)]
    for i in range(8):
        cols = slice(i * 512, (i + 1) * 512)
        acc = sum(jnp.dot(r, w_ref[h, cols], preferred_element_type=F32) for r, h in zip(rows, heads))
        own[:, cols] = acc[:64]
        for at, out in ((64, fwd_a), (96, fwd_b), (128, far_a), (160, far_b), (192, bwd_a), (224, bwd_b)):
            out[:, cols] = acc[at : at + 32].astype(out.dtype)


def output(where, mine, theirs, w):
    outs = [jax.ShapeDtypeStruct((64, 4096), F32)]
    outs += [jax.ShapeDtypeStruct((32, 4096), t) for t in (F32, BF, BF, F32, BF, BF)]
    return kernel_call(output_kernel, outs, where, mine, theirs, w)


def finish_kernel(where_ref, own, prev_a, prev_b, next_a, next_b, residual, gain, hidden, normed):
    for at, left, right in ((0, prev_a, next_a), (32, prev_b, next_b)):
        rows = slice(at, at + 32)
        x = residual[rows].astype(F32) + (own[rows] + (left[...].astype(F32) + right[...].astype(F32)))
        scale = lax.rsqrt(jnp.mean(x * x, -1, keepdims=True) + 1e-06)
        hidden[rows] = x.astype(BF)
        normed[rows] = (x * scale * gain[...]).astype(BF)


def finish(where, *args):
    return kernel_call(finish_kernel, [jax.ShapeDtypeStruct((64, 4096), BF)] * 2, where, *args)


def shards(memory, kv_weight, mem_lengths, queries, out_weight, residual, norm_gain):
    zh, x, yh, yl, zl, c = (lax.axis_index(a) for a in (Z, X, "yh", "yl", "zl", "c"))
    y = yh * 2 + yl
    where = jnp.stack([zh, x, y, c]).astype(jnp.int32)

    mine = pick(kv_weight[:, :512], kv_weight[:, 512:], c)
    theirs = pick(kv_weight[:, 512:], kv_weight[:, :512], c)
    w_c = swap(theirs, "c")
    w_z = swap(mine, "zl")
    w_zc = lax.ppermute(theirs, ("zl", "c"), [(i, 3 - i) for i in range(4)])
    rows = pair(pair(mine, w_c, c), pair(w_z, w_zc, c), zl)
    w_near = beyond(rows, X)
    w_near = jnp.stack([rows, *w_near])
    w_prev = lax.ppermute(w_near, Y, FWD)
    w_next = lax.ppermute(w_near, Y, BWD)
    w_far_a = lax.ppermute(w_prev[:2], Y, FWD)
    w_far_b = lax.ppermute(w_next[2:], Y, BWD)
    w_mine = jnp.concatenate([w_near, w_next, w_far_a, w_far_b, w_prev], 0).reshape((4,) + w_near.shape)
    w_theirs = swap(w_mine, "c")

    step = memory.shape[1] // 2
    half = 4 * step
    chunks = []
    for j in range(2):
        own = memory[:, j * step : (j + 1) * step].reshape(8 * step, 1024)
        prev = lax.ppermute(own, Z, FWD)
        nxt = lax.ppermute(own, Z, BWD)
        opp_a = lax.ppermute(prev[:half], Z, FWD)
        opp_b = lax.ppermute(nxt[half:], Z, BWD)
        chunks.append((own, nxt, opp_a, opp_b, prev))

    other = pick(queries[:, DH:], queries[:, :DH], c)
    other = swap(other, "c")
    q = pair(pick(queries[:, :DH], queries[:, DH:], c), other, c)
    other = swap(q, "zl")
    q = pair(q, other, zl)
    other = swap(q, "yl")
    q = pair(q, other, yl)

    length = lax.dynamic_index_in_dim(mem_lengths, x * 2 + yh, 0, keepdims=False)
    here = yl * 2 + zl
    here = jnp.stack([length, yl * 256 + zl * 128, here, here ^ 1, here ^ 2, here ^ 3]).astype(jnp.int32)
    state = None
    for j, pieces in enumerate(chunks):
        both = project(where, pieces, (w_mine, w_theirs))
        both = lax.all_to_all(both.reshape(16, step, 512), (X, "yh", "c"), 0, 0, tiled=True)
        state = attend(here, q, both.reshape(16 * step, 512), j, state)
    own, to_zl, to_yl, to_both = state

    parts = (
        own,
        swap(to_zl, "zl"),
        swap(to_yl, "yl"),
        lax.ppermute(to_both, ("yl", "zl"), [(i, 3 - i) for i in range(4)]),
    )
    mine, theirs = merge(where, parts)
    own, fwd_a, fwd_b, bwd_a, bwd_b, far_a, far_b = output(where, mine, swap(theirs, "c"), out_weight)

    far_a = lax.ppermute(far_a, Z, FWD)
    far_b = lax.ppermute(far_b, Z, BWD)
    prev_b = lax.ppermute(fwd_b, Z, FWD)
    next_a = lax.ppermute(bwd_a, Z, BWD)
    fwd_a = (fwd_a + far_a.astype(F32)).astype(BF)
    bwd_b = (bwd_b + far_b.astype(F32)).astype(BF)
    prev_a = lax.ppermute(fwd_a, Z, FWD)
    next_b = lax.ppermute(bwd_b, Z, BWD)
    return tuple(finish(where, own, prev_a, prev_b, next_a, next_b, residual, norm_gain.reshape(1, -1)))


def solution(mesh):
    fine = Mesh(mesh.devices.reshape(4, 4, 2, 2, 2, 2), (Z, X, "yh", "yl", "zl", "c"))
    seq = (X, "yh", "yl", "zl", "c")
    in_specs = (
        P(None, seq, Z),
        P(seq, Z),
        P(),
        P(seq, Z),
        P(Z, None),
        P(seq + (Z,), None),
        P(),
    )
    out_specs = (P(seq + (Z,), None), P(seq + (Z,), None))
    return jax.shard_map(shards, mesh=fine, in_specs=in_specs, out_specs=out_specs, check_vma=False)
```
